512 devices in a mesh: ctx: 32 (over x, y, core), head: 16 (over z).
Axes of the slice: x: 4, y: 4, z: 16, core: 2. Of those that a mesh axis runs over, the one named last changes fastest.
Arguments:
- mixed_in: bfloat16 [8192, 8192], P(('ctx', 'head')), may hold values from -6 to 6
- conv_weight: float32 [4, 8192], P(None, 'head'), may hold values from -3 to 3
- write_strength_logit: float32 [32, 8192], P('head', 'ctx'), may hold values from -10.5 to 2.2, as said below
- decay_log: float32 [32, 8192], P('head', 'ctx'), may hold values from -0.7 to 0, as said below
- initial_state: float32 [32, 128, 128], P('head'), may hold values from -6 to 6
- final_state_grad: float32 [32, 128, 128], P('head'), may hold values from -6 to 6
- grad_out: bfloat16 [8192, 4096], P('ctx', 'head'), may hold values from -6 to 6
Outputs:
- grad_mixed: bfloat16 [8192, 8192], P(('ctx', 'head'))
- grad_conv: float32 [4, 8192], P(None, 'head')
- grad_beta_logit: float32 [32, 8192], P('head', 'ctx')
- grad_decay_log: float32 [32, 8192], P('head', 'ctx')
The draws below stay inside these ranges and needn't reach their ends.
Inputs may be any that keep to these rules, and one draw needn't show every extreme that they name: `write_strength_logit`: each value head's write strengths and decays vary from token to token. `decay_log`: every entry is negative.
All inputs are finite; a program needn't handle non-finite values.
Results may differ from the reference program's by a relative error of at most 0.001.
Values may be sent and summed in bfloat16 or wider, within the bound.
A program may use at most 64 MiB of HBM per device.

```python
import math
import jax
import jax.numpy as jnp
from jax import lax

HK = 16
VALUE_HEADS = 32
DK = 128
DV = 128
KW = 4
BLOCK = 64
SLAB_TOKENS = 8192
CH = 8192


def keeping_heads(key):
    share = 0.5
    return jax.random.uniform(jax.random.fold_in(key, 7), (VALUE_HEADS, 1)) < share


def roughness(key):
    return jnp.exp(jax.random.uniform(key, (VALUE_HEADS, SLAB_TOKENS), minval=-0.7, maxval=0.7))


def draw_write_strength_logit(key, part):
    keeping = keeping_heads(key)
    first = jax.random.fold_in(key, 11)
    second = jax.random.fold_in(key, 12)
    level = jnp.exp(jax.random.uniform(first, (VALUE_HEADS, 1), minval=math.log(0.05), maxval=math.log(0.5)))
    strength = jnp.where(keeping, level * DK / SLAB_TOKENS, level)
    strength = jnp.minimum(strength * roughness(second), 0.9)
    return (jnp.log(strength) - jnp.log1p(-strength)).astype(jnp.float32)


def draw_decay_log(key, part):
    keeping = keeping_heads(key)
    first = jax.random.fold_in(key, 21)
    second = jax.random.fold_in(key, 22)
    third = jax.random.fold_in(key, 23)
    fourth = jax.random.fold_in(key, 24)
    fifth_piece = jax.random.fold_in(key, 25)
    slow_rate = jnp.exp(jax.random.uniform(first, (VALUE_HEADS, 1), minval=math.log(0.02), maxval=math.log(0.3))) / SLAB_TOKENS
    fast_rate = 1.0 / jax.random.uniform(second, (VALUE_HEADS, 1), minval=30.0, maxval=50.0)
    rate = jnp.where(keeping, slow_rate, fast_rate)
    smoothed_signal = -rate * roughness(third)
    spots = jax.random.randint(fourth, (VALUE_HEADS, 3, 1), 0, SLAB_TOKENS)
    positions = jnp.arange(SLAB_TOKENS, dtype=jnp.int32)[None, None, :]
    matched_entry = jnp.any(positions == spots, axis=1)
    sudden_spike = jnp.log(jax.random.uniform(fifth_piece, (VALUE_HEADS, SLAB_TOKENS), minval=0.5, maxval=0.8))
    return jnp.where(matched_entry, sudden_spike, smoothed_signal).astype(jnp.float32)


def block_scale(rng, dims, cuts, least, top_value):
    level = 1.0
    for dim, shards_of in cuts:
        draws = jax.random.uniform(jax.random.fold_in(jax.random.fold_in(rng, 6), dim), (shards_of,), jnp.float32, least / len(cuts), top_value / len(cuts))
        level = level * jnp.repeat(jnp.exp(draws), dims[dim] // shards_of).reshape((-1,) + (1,) * (len(dims) - 1 - dim))
    return level


def normal_values(key, extent, scale, reach, cuts=(), held_as=jnp.bfloat16):
    loudness = block_scale(key, extent, cuts, -0.22, 0.18) if cuts else 1.0
    entries = jax.random.normal(key, extent, jnp.float32) * scale * loudness
    return jnp.minimum(jnp.maximum(entries, -reach), reach).astype(held_as)


def setup_inputs(seed: int = 0) -> dict:
    arg_keys = jax.random.split(jax.random.key(seed), 8)
    mixed_in = normal_values(arg_keys[0], (SLAB_TOKENS, CH), 1.0, 6.0, ((0, 512),))
    conv_weight = normal_values(arg_keys[1], (KW, CH), KW ** -0.5, 3.0, ((1, 16),), jnp.float32)
    write_strength_logit = draw_write_strength_logit(jax.random.fold_in(arg_keys[7], 71), 0)
    decay_log = draw_decay_log(jax.random.fold_in(arg_keys[7], 71), 0)
    initial_state = normal_values(arg_keys[4], (VALUE_HEADS, DK, DV), 1.0, 6.0, ((0, 16),), jnp.float32)
    final_state_grad = normal_values(arg_keys[5], (VALUE_HEADS, DK, DV), 1.0, 6.0, ((0, 16),), jnp.float32)
    grad_out = normal_values(arg_keys[6], (SLAB_TOKENS, VALUE_HEADS * DV), 1.0, 6.0, ((0, 32), (1, 16)))
    return {"mixed_in": mixed_in, "conv_weight": conv_weight, "write_strength_logit": write_strength_logit, "decay_log": decay_log, "initial_state": initial_state, "final_state_grad": final_state_grad, "grad_out": grad_out}


highest = lax.Precision.HIGHEST
norm_eps = 1e-06

def block_step(carried, pieces):
    state, transit = carried
    queries, key_feats, values, beta_gate, log_decay = pieces
    block_size = log_decay.shape[0]
    cumulative = jnp.cumsum(log_decay)
    row_ids = lax.broadcasted_iota(jnp.int32, (block_size, block_size), 0)
    col_ids = lax.broadcasted_iota(jnp.int32, (block_size, block_size), 1)
    causal = col_ids <= row_ids
    differ = jnp.where(causal, cumulative[:, None] - cumulative[None, :], 0.0)
    ratios = jnp.where(causal, jnp.exp(differ), 0.0)
    key_gram = jnp.dot(key_feats, key_feats.T, precision=highest)
    lower_part = jnp.where(col_ids < row_ids, beta_gate[:, None] * ratios * key_gram, 0.0)
    system = lower_part + jnp.eye(block_size, dtype=jnp.float32)
    decays = jnp.exp(cumulative)
    right_sides = jnp.concatenate([beta_gate[:, None] * values, (beta_gate * decays)[:, None] * key_feats], axis=1)
    solved = jax.scipy.linalg.solve_triangular(system, right_sides, lower=True)
    width_v = values.shape[1]
    base_update = solved[:, :width_v]
    weights = solved[:, width_v:]
    update = base_update - jnp.dot(weights, state, precision=highest)
    scores = ratios * jnp.dot(queries, key_feats.T, precision=highest)
    output = decays[:, None] * jnp.dot(queries, state, precision=highest) + jnp.dot(scores, update, precision=highest)
    total_decay = jnp.exp(cumulative[-1])
    tail_keys = jnp.exp(cumulative[-1] - cumulative)[:, None] * key_feats
    new_state = total_decay * state + jnp.dot(tail_keys.T, update, precision=highest)
    step_map = total_decay * jnp.eye(key_feats.shape[1], dtype=jnp.float32) - jnp.dot(tail_keys.T, weights, precision=highest)
    new_transit = jnp.dot(step_map, transit, precision=highest)
    return ((new_state, new_transit), output)

def run_head(state, queries, key_feats, values, beta_gate, log_decay):
    blocks = queries.shape[0] // BLOCK
    pieces = (queries.reshape(blocks, BLOCK, -1), key_feats.reshape(blocks, BLOCK, -1), values.reshape(blocks, BLOCK, -1), beta_gate.reshape(blocks, BLOCK), log_decay.reshape(blocks, BLOCK))
    start = (state, jnp.eye(key_feats.shape[1], dtype=jnp.float32))
    (state_end, transit), outputs = lax.scan(jax.checkpoint(block_step), start, pieces)
    return (outputs.reshape(-1, values.shape[1]), state_end, transit)

def normalize(feats, factor):
    return feats * lax.rsqrt(lax.optimization_barrier(jnp.sum(feats * feats, axis=-1, keepdims=True)) + norm_eps) * factor

def mix_layer(state_in, extended, conv_weight, write_strength_logit, decay_log):
    row_count = extended.shape[0] - (KW - 1)
    filtered_signal = conv_weight[0] * extended[0:row_count]
    for tap in range(1, KW):
        filtered_signal = filtered_signal + conv_weight[tap] * extended[tap:tap + row_count]
    activated = jax.nn.silu(filtered_signal)
    ratio_heads = VALUE_HEADS // HK
    group_width = 2 * DK + ratio_heads * DV
    groups = activated.reshape(row_count, -1, group_width)
    key_heads = groups.shape[1]
    queries = normalize(groups[:, :, :DK], DK ** (-0.5))
    key_feats = normalize(groups[:, :, DK:2 * DK], 1.0)
    values = groups[:, :, 2 * DK:].reshape(row_count, key_heads * ratio_heads, DV).transpose(1, 0, 2)
    queries = jnp.repeat(queries.transpose(1, 0, 2), ratio_heads, axis=0)
    key_feats = jnp.repeat(key_feats.transpose(1, 0, 2), ratio_heads, axis=0)
    beta_gate = jax.nn.sigmoid(write_strength_logit)
    outputs, state_out, transit = jax.vmap(run_head)(state_in, queries, key_feats, values, beta_gate, decay_log)
    result = outputs.transpose(1, 0, 2).reshape(row_count, -1)
    return ((result, state_out), transit)

def reference(mixed_in, conv_weight, write_strength_logit, decay_log, initial_state, final_state_grad, grad_out):
    extended = jnp.concatenate([jnp.zeros((KW - 1, mixed_in.shape[1]), jnp.float32), mixed_in.astype(jnp.float32)], axis=0)

    def forward(ext_rows, weight_taps, logits, decay_logs):
        return mix_layer(initial_state, ext_rows, weight_taps, logits, decay_logs)
    primal, pull_all, transit = jax.vjp(forward, extended, conv_weight, write_strength_logit, decay_log, has_aux=True)
    grads = pull_all((grad_out.astype(jnp.float32), final_state_grad))
    return (grads[0][KW - 1:].astype(jnp.bfloat16), grads[1], grads[2], grads[3])
```

```python
import functools
import jax
import jax.numpy as jnp
from jax import lax
from jax.experimental import pallas as pl
from jax.experimental.pallas import tpu as pltpu
from jax.sharding import PartitionSpec as P

DK = 128
DV = 128
KW = 4
EDGE = 16

f32 = jnp.float32
bf16 = jnp.bfloat16
highest = lax.Precision.HIGHEST
norm_eps = 1e-06


def split(a):
    hi = a.astype(bf16)
    return (hi, (a - hi.astype(f32)).astype(bf16))


def dot(a, b, ca, cb):
    return lax.dot_general(a, b, (((ca,), (cb,)), ((), ())), preferred_element_type=f32)


def mm(a, b, ca=1, cb=0):
    out = dot(a[0], b[0], ca, cb)
    if len(b) > 1:
        out = out + dot(a[0], b[1], ca, cb)
    if len(a) > 1:
        out = out + dot(a[1], b[0], ca, cb)
    return out


def activate(ext, x_ref, edge_ref, w_ref):
    rows = x_ref.shape[0]
    ext[0:EDGE, :] = edge_ref[...].astype(f32)
    ext[EDGE : EDGE + rows, :] = x_ref[...].astype(f32)
    conv = w_ref[KW - 1 : KW, :] * ext[EDGE : EDGE + rows, :]
    for tap in range(KW - 1):
        at = EDGE - (KW - 1) + tap
        conv = conv + w_ref[tap : tap + 1, :] * ext[at : at + rows, :]
    sig = 1.0 / (1.0 + jnp.exp(-conv))
    return conv, sig, conv * sig


def inv_norm(a):
    return lax.rsqrt(jnp.sum(a * a, axis=-1, keepdims=True) + norm_eps)


def gates(logit_ref, g_ref):
    heads, rows = g_ref.shape
    i = lax.broadcasted_iota(jnp.int32, (rows, rows), 0)
    j = lax.broadcasted_iota(jnp.int32, (rows, rows), 1)
    upto = jnp.where(i <= j, 1.0, 0.0).astype(bf16)
    g = g_ref[...]
    g1 = g.astype(bf16)
    rest = g - g1.astype(f32)
    g2 = rest.astype(bf16)
    g3 = (rest - g2.astype(f32)).astype(bf16)
    c_row = (dot(g3, upto, 1, 0) + dot(g2, upto, 1, 0)) + dot(g1, upto, 1, 0)
    b_row = 1.0 / (1.0 + jnp.exp(-logit_ref[...]))
    pad = jnp.zeros((8 - 2 * heads, rows), f32)
    cols = jnp.concatenate([c_row, b_row, pad], axis=0).T
    return c_row, b_row, cols, i, j


def ratios_of(c_col, c_row, i, j):
    return jnp.where(j <= i, jnp.exp(jnp.where(j <= i, c_col - c_row, 0.0)), 0.0)


def invert_unit_lower(low, n):
    i = lax.broadcasted_iota(jnp.int32, (n, n), 0)
    j = lax.broadcasted_iota(jnp.int32, (n, n), 1)
    eye = jnp.where(i == j, 1.0, 0.0)
    inv = [eye - jnp.where((i ^ j) == 1, part, 0.0) for part in low]
    shift = 1
    while (1 << shift) < n:
        pick = ((i >> shift) ^ (j >> shift)) == 1
        parts = [split(a) for a in inv]
        mid = [
            mm(p, split(jnp.where(pick, part, 0.0))) for p, part in zip(parts, low)
        ]
        inv = [a - mm(split(m), p) for a, m, p in zip(inv, mid, parts)]
        shift += 1
    return inv


def prepare_kernel(
    x_ref, edge_ref, w_ref, logit_ref, g_ref, do_ref,
    at_ref, bt_ref, ct_ref, solve_ref, base_ref, weight_ref, score_ref, gram_ref,
    ext,
):
    heads, rows = g_ref.shape
    half = rows // 2
    _, _, act = activate(ext, x_ref, edge_ref, w_ref)
    a, b = act[:, :DK], act[:, DK : 2 * DK]
    q = a * (inv_norm(a) * DK**-0.5)
    k = b * inv_norm(b)
    qs, ks = split(q), split(k)
    gram = mm(ks, ks, 1, 1)
    qk = mm(qs, ks, 1, 1)
    c_row, b_row, cols, i, j = gates(logit_ref, g_ref)
    lows = []
    for h in range(heads):
        ratios = ratios_of(cols[:, h : h + 1], c_row[h : h + 1, :], i, j)
        rg = jnp.where(j < i, ratios * gram, 0.0)
        gram_ref[h] = rg
        score_ref[h] = ratios * qk
        lows.append(cols[:, heads + h : heads + h + 1] * rg)
    diag = []
    for low in lows:
        diag += [low[:half, :half], low[half:, half:]]
    diag = invert_unit_lower(diag, half)
    for h in range(heads):
        first, second = split(diag[2 * h]), split(diag[2 * h + 1])
        corner = mm(split(mm(second, split(lows[h][half:, :half]))), first)
        solve_ref[h, :half, :half] = diag[2 * h]
        solve_ref[h, :half, half:] = jnp.zeros((half, half), f32)
        solve_ref[h, half:, :half] = -corner
        solve_ref[h, half:, half:] = diag[2 * h + 1]
        c_col = cols[:, h : h + 1]
        b_col = cols[:, heads + h : heads + h + 1]
        decays = jnp.exp(c_col)
        last = c_col[rows - 1 : rows, :]
        v = act[:, 2 * DK + h * DV : 2 * DK + (h + 1) * DV]
        right = jnp.concatenate([b_col * v, (b_col * decays) * k], axis=1)
        solved = mm(split(solve_ref[h]), split(right))
        base, weights = solved[:, :DV], solved[:, DV:]
        base_ref[h] = base
        weight_ref[h] = weights
        tail = split(jnp.exp(last - c_col) * k)
        wide = mm(split(solved), tail, 0, 0)
        ii = lax.broadcasted_iota(jnp.int32, (DK, DK), 0)
        jj = lax.broadcasted_iota(jnp.int32, (DK, DK), 1)
        bt_ref[h] = wide[:DV]
        at_ref[h] = jnp.where(ii == jj, jnp.exp(last), 0.0) - wide[DV:]
        reach = decays * q - mm(split(score_ref[h]), split(weights))
        ct_ref[h] = mm((do_ref[:, h * DV : (h + 1) * DV],), split(reach), 0, 0)


def backward_kernel(
    x_ref, edge_ref, w_ref, logit_ref, g_ref, do_ref,
    solve_ref, base_ref, weight_ref, score_ref, gram_ref, st_ref, dst_ref,
    own_ref, last_ref, spill_ref, gw_ref, glogit_ref, gdecay_ref,
    ext, dext,
):
    heads, rows = g_ref.shape
    conv, sig, act = activate(ext, x_ref, edge_ref, w_ref)
    a, b = act[:, :DK], act[:, DK : 2 * DK]
    qr, kr = inv_norm(a), inv_norm(b)
    q = a * (qr * DK**-0.5)
    k = b * kr
    qs, ks = split(q), split(k)
    c_row, b_row, cols, i, j = gates(logit_ref, g_ref)
    lower = j < i
    dq = None
    row_terms, col_terms = [], []
    for h in range(heads):
        c_col = cols[:, h : h + 1]
        b_col = cols[:, heads + h : heads + h + 1]
        decays = jnp.exp(c_col)
        last = c_col[rows - 1 : rows, :]
        tail = jnp.exp(last - c_col)
        ratios = ratios_of(c_col, c_row[h : h + 1, :], i, j)
        v = act[:, 2 * DK + h * DV : 2 * DK + (h + 1) * DV]
        do = do_ref[:, h * DV : (h + 1) * DV]
        st, dst = st_ref[h], dst_ref[h]
        sts, dsts = split(st), split(dst)
        tail_k = tail * k
        update = base_ref[h] - mm(split(weight_ref[h]), sts, 1, 1)
        score = score_ref[h]
        d_update = mm(split(score), (do,), 0, 0) + mm(split(tail_k), dsts, 1, 1)
        x = mm(split(solve_ref[h]), split(d_update), 0, 0)
        us, xs = split(update), split(x)
        d_score = mm((do,), us, 1, 1)
        d_low = -mm(xs, us, 1, 1)
        do_s = mm((do,), sts)
        y = -mm(xs, sts)
        d_tail = mm(us, dsts)
        z = ratios * d_score
        rg = gram_ref[h]
        rgd = rg * d_low
        d_gram = jnp.where(lower, b_col * (ratios * d_low), 0.0)
        part_q = decays * do_s
        part_k = tail * d_tail + (b_col * decays) * y
        if dq is None:
            dq, dk, zs, dgs = part_q, part_k, z, d_gram
        else:
            dq, dk, zs, dgs = dq + part_q, dk + part_k, zs + z, dgs + d_gram
        flow = jnp.where(lower, score * d_score, 0.0) + b_col * rgd
        yk = decays * jnp.sum(y * k, axis=1, keepdims=True)
        tk = jnp.sum(tail_k * d_tail, axis=1, keepdims=True)
        d_beta = (
            jnp.sum(x * v, axis=1, keepdims=True)
            + yk
            + jnp.sum(rgd, axis=1, keepdims=True)
        )
        d_cum = (
            jnp.sum(flow, axis=1, keepdims=True)
            + jnp.sum(q * part_q, axis=1, keepdims=True)
            + b_col * yk
            - tk
        )
        ends = jnp.exp(last) * jnp.sum(dst * st, keepdims=True) + jnp.sum(tk, keepdims=True)
        at_end = lax.broadcasted_iota(jnp.int32, (rows, 1), 0) == rows - 1
        d_cum = d_cum + jnp.where(at_end, ends, 0.0)
        row_terms.append(jnp.sum(flow, axis=0, keepdims=True))
        col_terms.append((d_cum, d_beta))
        s = sig[:, 2 * DK + h * DV : 2 * DK + (h + 1) * DV]
        c = conv[:, 2 * DK + h * DV : 2 * DK + (h + 1) * DV]
        dext[EDGE : EDGE + rows, 2 * DK + h * DV : 2 * DK + (h + 1) * DV] = (
            (b_col * x) * (s * (1.0 + c * (1.0 - s)))
        )
    zs, dgs = split(zs), split(dgs)
    dq = dq + mm(zs, ks)
    dk = dk + mm(zs, qs, 0, 0) + mm(dgs, ks) + mm(dgs, ks, 0, 0)
    for at, value, inv, d, factor in ((0, a, qr, dq, DK**-0.5), (DK, b, kr, dk, 1.0)):
        inner = jnp.sum(value * d, axis=1, keepdims=True)
        d_act = (inv * factor) * (d - value * (inv * inv * inner))
        s, c = sig[:, at : at + DK], conv[:, at : at + DK]
        dext[EDGE : EDGE + rows, at : at + DK] = d_act * (s * (1.0 + c * (1.0 - s)))
    width = dext.shape[1]
    dext[0:EDGE, :] = jnp.zeros((EDGE, width), f32)
    dext[EDGE + rows :, :] = jnp.zeros((dext.shape[0] - EDGE - rows, width), f32)
    own = w_ref[KW - 1 : KW, :] * dext[EDGE : EDGE + rows, :]
    at = EDGE - (EDGE - KW + 1)
    spill = w_ref[KW - 1 : KW, :] * dext[0:EDGE, :]
    for tap in range(KW):
        back = KW - 1 - tap
        if back:
            own = own + w_ref[tap : tap + 1, :] * dext[EDGE + back : EDGE + back + rows, :]
            spill = spill + w_ref[tap : tap + 1, :] * dext[back : back + EDGE, :]
    own_ref[...] = own.astype(bf16)
    last_ref[...] = own[rows - EDGE :, :]
    spill_ref[...] = spill
    d_conv = dext[EDGE : EDGE + rows, :]
    for tap in range(KW):
        at = EDGE - (KW - 1) + tap
        gw_ref[tap : tap + 1, :] = jnp.sum(d_conv * ext[at : at + rows, :], axis=0, keepdims=True)
    lanes = lax.broadcasted_iota(jnp.int32, (rows, 8), 1)
    packed = jnp.zeros((rows, 8), f32)
    for h in range(heads):
        packed = jnp.where(lanes == h, col_terms[h][0], packed)
        packed = jnp.where(lanes == heads + h, col_terms[h][1], packed)
    packed = packed.T
    glogit_ref[...] = packed[heads : 2 * heads] * b_row * (1.0 - b_row)
    d_cum = packed[:heads] - jnp.concatenate(row_terms, axis=0)
    onward = jnp.where(i >= j, 1.0, 0.0).astype(bf16)
    d1 = d_cum.astype(bf16)
    rest = d_cum - d1.astype(f32)
    d2 = rest.astype(bf16)
    d3 = (rest - d2.astype(f32)).astype(bf16)
    gdecay_ref[...] = (dot(d3, onward, 1, 0) + dot(d2, onward, 1, 0)) + dot(d1, onward, 1, 0)


def shape_of(*extent, dtype=f32):
    return jax.ShapeDtypeStruct(extent, dtype)


def prepare(x, edge, w, logits, g, do):
    rows, width = x.shape
    heads = g.shape[0]
    return pl.pallas_call(
        prepare_kernel,
        out_shape=(
            shape_of(heads, DK, DK),
            shape_of(heads, DV, DK),
            shape_of(heads, DV, DK),
            shape_of(heads, rows, rows),
            shape_of(heads, rows, DV),
            shape_of(heads, rows, DK),
            shape_of(heads, rows, rows),
            shape_of(heads, rows, rows),
        ),
        scratch_shapes=[pltpu.VMEM((EDGE + rows, width), f32)],
        compiler_params=pltpu.CompilerParams(vmem_limit_bytes=48 << 20),
        name="prepare",
    )(x, edge, w, logits, g, do)


def backward(x, edge, w, logits, g, do, solve, base, weights, score, gram, st, dst):
    rows, width = x.shape
    heads = g.shape[0]
    return pl.pallas_call(
        backward_kernel,
        out_shape=(
            shape_of(rows, width, dtype=bf16),
            shape_of(EDGE, width),
            shape_of(EDGE, width),
            shape_of(KW, width),
            shape_of(heads, rows),
            shape_of(heads, rows),
        ),
        scratch_shapes=[
            pltpu.VMEM((EDGE + rows, width), f32),
            pltpu.VMEM((2 * EDGE + rows, width), f32),
        ],
        compiler_params=pltpu.CompilerParams(vmem_limit_bytes=48 << 20),
        name="backward",
    )(x, edge, w, logits, g, do, solve, base, weights, score, gram, st, dst)


def from_behind(value, axis, by):
    devices = lax.axis_size(axis)
    pairs = [(i, i + by) for i in range(devices) if 0 <= i + by < devices]
    return lax.ppermute(value, axis, pairs)


def scan_states(at, bt, ct, initial_state, final_state_grad):
    devices, mine = lax.axis_size("ctx"), lax.axis_index("ctx")
    ein = functools.partial(jnp.einsum, precision=highest)

    def sweep(m, o, start, way):
        first = 0 if way > 0 else devices - 1
        o = jnp.where(mine == first, ein("hvi,hij->hvj", start, m) + o, o)
        by = 1
        while by < devices:
            mo, oo = from_behind((m, o), "ctx", way * by)
            has = (mine >= by) if way > 0 else (mine < devices - by)
            o = jnp.where(has, ein("hvi,hij->hvj", oo, m) + o, o)
            m = jnp.where(has, ein("hki,hij->hkj", mo, m), m)
            by *= 2
        return jnp.where(mine == first, start, from_behind(o, "ctx", way))

    st = sweep(at, bt, jnp.swapaxes(initial_state, 1, 2), 1)
    dst = sweep(jnp.swapaxes(at, 1, 2), ct, jnp.swapaxes(final_state_grad, 1, 2), -1)
    return st, dst


def on_device(mixed_in, conv_weight, logits, decay_log, initial_state, final_state_grad, grad_out):
    x = lax.all_to_all(mixed_in, "head", split_axis=1, concat_axis=0, tiled=True)
    edge = from_behind(x[-EDGE:], "ctx", 1)
    at, bt, ct, *kept = prepare(x, edge, conv_weight, logits, decay_log, grad_out)
    st, dst = scan_states(at, bt, ct, initial_state, final_state_grad)
    own, last, spill, gw, glogit, gdecay = backward(
        x, edge, conv_weight, logits, decay_log, grad_out, *kept, st, dst
    )
    last = (last + from_behind(spill, "ctx", -1)).astype(bf16)
    own = jnp.concatenate([own[:-EDGE], last], axis=0)
    returned = lax.all_to_all(own, "head", split_axis=0, concat_axis=1, tiled=True)
    return (returned, lax.psum(gw, "ctx"), glogit, gdecay)


def solution(mesh):
    in_specs = (
        P(("ctx", "head"), None),
        P(None, "head"),
        P("head", "ctx"),
        P("head", "ctx"),
        P("head", None, None),
        P("head", None, None),
        P("ctx", "head"),
    )
    out_specs = (P(("ctx", "head"), None), P(None, "head"), P("head", "ctx"), P("head", "ctx"))
    return jax.shard_map(
        on_device, mesh=mesh, in_specs=in_specs, out_specs=out_specs, check_vma=False
    )
```

```python
import functools
import jax
import jax.numpy as jnp
from jax import lax
from jax.experimental import pallas as pl
from jax.experimental.pallas import tpu as pltpu
from jax.sharding import PartitionSpec as P

DK = 128
DV = 128
KW = 4
EDGE = 16

f32 = jnp.float32
bf16 = jnp.bfloat16
norm_eps = 1e-06


def split(a):
    hi = a.astype(bf16)
    return (hi, (a - hi.astype(f32)).astype(bf16))


def dot(a, b, ca, cb):
    return lax.dot_general(a, b, (((ca,), (cb,)), ((), ())), preferred_element_type=f32)


def mm(a, b, ca=1, cb=0):
    out = dot(a[0], b[0], ca, cb)
    if len(b) > 1:
        out = out + dot(a[0], b[1], ca, cb)
    if len(a) > 1:
        out = out + dot(a[1], b[0], ca, cb)
    return out


def activate(ext, x_ref, edge_ref, w_ref):
    rows = x_ref.shape[0]
    ext[0:EDGE, :] = jnp.where(lax.axis_index("ctx") > 0, edge_ref[...].astype(f32), 0.0)
    ext[EDGE : EDGE + rows, :] = x_ref[...].astype(f32)
    conv = w_ref[KW - 1 : KW, :] * ext[EDGE : EDGE + rows, :]
    for tap in range(KW - 1):
        at = EDGE - (KW - 1) + tap
        conv = conv + w_ref[tap : tap + 1, :] * ext[at : at + rows, :]
    sig = 1.0 / (1.0 + jnp.exp(-conv))
    return conv, sig, conv * sig


def inv_norm(a):
    return lax.rsqrt(jnp.sum(a * a, axis=-1, keepdims=True) + norm_eps)


def gates(logit_ref, g_ref):
    heads, rows = g_ref.shape
    i = lax.broadcasted_iota(jnp.int32, (rows, rows), 0)
    j = lax.broadcasted_iota(jnp.int32, (rows, rows), 1)
    upto = jnp.where(i <= j, 1.0, 0.0).astype(bf16)
    g = g_ref[...]
    g1 = g.astype(bf16)
    rest = g - g1.astype(f32)
    g2 = rest.astype(bf16)
    g3 = (rest - g2.astype(f32)).astype(bf16)
    c_row = (dot(g3, upto, 1, 0) + dot(g2, upto, 1, 0)) + dot(g1, upto, 1, 0)
    b_row = 1.0 / (1.0 + jnp.exp(-logit_ref[...]))
    pad = jnp.zeros((8 - 2 * heads, rows), f32)
    cols = jnp.concatenate([c_row, b_row, pad], axis=0).T
    return c_row, b_row, cols, i, j


def ratios_of(c_col, c_row, i, j):
    return jnp.where(j <= i, jnp.exp(jnp.where(j <= i, c_col - c_row, 0.0)), 0.0)


def invert_unit_lower(low, n):
    i = lax.broadcasted_iota(jnp.int32, (n, n), 0)
    j = lax.broadcasted_iota(jnp.int32, (n, n), 1)
    eye = jnp.where(i == j, 1.0, 0.0)
    inv = [eye - jnp.where((i ^ j) == 1, part, 0.0) for part in low]
    shift = 1
    while (1 << shift) < n:
        pick = ((i >> shift) ^ (j >> shift)) == 1
        parts = [split(a) for a in inv]
        mid = [
            mm(p, split(jnp.where(pick, part, 0.0))) for p, part in zip(parts, low)
        ]
        inv = [a - mm(split(m), p) for a, m, p in zip(inv, mid, parts)]
        shift += 1
    return inv


def prepare_kernel(
    x_ref, edge_ref, w_ref, logit_ref, g_ref, do_ref,
    maps_ref, solve_ref, base_ref, weight_ref, score_ref, gram_ref,
    ext,
):
    heads, rows = g_ref.shape
    half = rows // 2
    _, _, act = activate(ext, x_ref, edge_ref, w_ref)
    a, b = act[:, :DK], act[:, DK : 2 * DK]
    q = a * (inv_norm(a) * DK**-0.5)
    k = b * inv_norm(b)
    qs, ks = split(q), split(k)
    gram = mm(ks, ks, 1, 1)
    qk = mm(qs, ks, 1, 1)
    c_row, b_row, cols, i, j = gates(logit_ref, g_ref)
    lows = []
    for h in range(heads):
        ratios = ratios_of(cols[:, h : h + 1], c_row[h : h + 1, :], i, j)
        rg = jnp.where(j < i, ratios * gram, 0.0)
        gram_ref[h] = rg
        score_ref[h] = ratios * qk
        lows.append(cols[:, heads + h : heads + h + 1] * rg)
    diag = []
    for low in lows:
        diag += [low[:half, :half], low[half:, half:]]
    diag = invert_unit_lower(diag, half)
    for h in range(heads):
        first, second = split(diag[2 * h]), split(diag[2 * h + 1])
        corner = mm(split(mm(second, split(lows[h][half:, :half]))), first)
        solve_ref[h, :half, :half] = diag[2 * h]
        solve_ref[h, :half, half:] = jnp.zeros((half, half), f32)
        solve_ref[h, half:, :half] = -corner
        solve_ref[h, half:, half:] = diag[2 * h + 1]
        c_col = cols[:, h : h + 1]
        b_col = cols[:, heads + h : heads + h + 1]
        decays = jnp.exp(c_col)
        last = c_col[rows - 1 : rows, :]
        v = act[:, 2 * DK + h * DV : 2 * DK + (h + 1) * DV]
        right = jnp.concatenate([b_col * v, (b_col * decays) * k], axis=1)
        solved = mm(split(solve_ref[h]), split(right))
        base, weights = solved[:, :DV], solved[:, DV:]
        base_ref[h] = base
        weight_ref[h] = weights
        tail = split(jnp.exp(last - c_col) * k)
        wide = mm(split(solved), tail, 0, 0)
        ii = lax.broadcasted_iota(jnp.int32, (DK, DK), 0)
        jj = lax.broadcasted_iota(jnp.int32, (DK, DK), 1)
        maps_ref[h, 1] = wide[:DV]
        maps_ref[h, 0] = jnp.where(ii == jj, jnp.exp(last), 0.0) - wide[DV:]
        reach = decays * q - mm(split(score_ref[h]), split(weights))
        maps_ref[h, 2] = mm((do_ref[:, h * DV : (h + 1) * DV],), split(reach), 0, 0)


def backward_kernel(
    x_ref, edge_ref, w_ref, logit_ref, g_ref, do_ref,
    solve_ref, base_ref, weight_ref, score_ref, gram_ref, state_ref,
    own_ref, last_ref, spill_ref, gw_ref, glogit_ref, gdecay_ref,
    ext, dext,
):
    heads, rows = g_ref.shape
    conv, sig, act = activate(ext, x_ref, edge_ref, w_ref)
    a, b = act[:, :DK], act[:, DK : 2 * DK]
    qr, kr = inv_norm(a), inv_norm(b)
    q = a * (qr * DK**-0.5)
    k = b * kr
    qs, ks = split(q), split(k)
    c_row, b_row, cols, i, j = gates(logit_ref, g_ref)
    lower = j < i
    dq = None
    row_terms, col_terms = [], []
    for h in range(heads):
        c_col = cols[:, h : h + 1]
        b_col = cols[:, heads + h : heads + h + 1]
        decays = jnp.exp(c_col)
        last = c_col[rows - 1 : rows, :]
        tail = jnp.exp(last - c_col)
        ratios = ratios_of(c_col, c_row[h : h + 1, :], i, j)
        v = act[:, 2 * DK + h * DV : 2 * DK + (h + 1) * DV]
        do = do_ref[:, h * DV : (h + 1) * DV]
        st, dst = state_ref[h, 0], state_ref[h, 1]
        sts, dsts = split(st), split(dst)
        tail_k = tail * k
        update = base_ref[h] - mm(split(weight_ref[h]), sts, 1, 1)
        score = score_ref[h]
        d_update = mm(split(score), (do,), 0, 0) + mm(split(tail_k), dsts, 1, 1)
        x = mm(split(solve_ref[h]), split(d_update), 0, 0)
        us, xs = split(update), split(x)
        d_score = mm((do,), us, 1, 1)
        d_low = -mm(xs, us, 1, 1)
        do_s = mm((do,), sts)
        y = -mm(xs, sts)
        d_tail = mm(us, dsts)
        z = ratios * d_score
        rg = gram_ref[h]
        rgd = rg * d_low
        d_gram = jnp.where(lower, b_col * (ratios * d_low), 0.0)
        part_q = decays * do_s
        part_k = tail * d_tail + (b_col * decays) * y
        if dq is None:
            dq, dk, zs, dgs = part_q, part_k, z, d_gram
        else:
            dq, dk, zs, dgs = dq + part_q, dk + part_k, zs + z, dgs + d_gram
        flow = jnp.where(lower, score * d_score, 0.0) + b_col * rgd
        yk = decays * jnp.sum(y * k, axis=1, keepdims=True)
        tk = jnp.sum(tail_k * d_tail, axis=1, keepdims=True)
        d_beta = (
            jnp.sum(x * v, axis=1, keepdims=True)
            + yk
            + jnp.sum(rgd, axis=1, keepdims=True)
        )
        d_cum = (
            jnp.sum(flow, axis=1, keepdims=True)
            + jnp.sum(q * part_q, axis=1, keepdims=True)
            + b_col * yk
            - tk
        )
        ends = jnp.exp(last) * jnp.sum(dst * st, keepdims=True) + jnp.sum(tk, keepdims=True)
        at_end = lax.broadcasted_iota(jnp.int32, (rows, 1), 0) == rows - 1
        d_cum = d_cum + jnp.where(at_end, ends, 0.0)
        row_terms.append(jnp.sum(flow, axis=0, keepdims=True))
        col_terms.append((d_cum, d_beta))
        s = sig[:, 2 * DK + h * DV : 2 * DK + (h + 1) * DV]
        c = conv[:, 2 * DK + h * DV : 2 * DK + (h + 1) * DV]
        dext[EDGE : EDGE + rows, 2 * DK + h * DV : 2 * DK + (h + 1) * DV] = (
            (b_col * x) * (s * (1.0 + c * (1.0 - s)))
        )
    zs, dgs = split(zs), split(dgs)
    dq = dq + mm(zs, ks)
    dk = dk + mm(zs, qs, 0, 0) + mm(dgs, ks) + mm(dgs, ks, 0, 0)
    for at, value, inv, d, factor in ((0, a, qr, dq, DK**-0.5), (DK, b, kr, dk, 1.0)):
        inner = jnp.sum(value * d, axis=1, keepdims=True)
        d_act = (inv * factor) * (d - value * (inv * inv * inner))
        s, c = sig[:, at : at + DK], conv[:, at : at + DK]
        dext[EDGE : EDGE + rows, at : at + DK] = d_act * (s * (1.0 + c * (1.0 - s)))
    width = dext.shape[1]
    dext[0:EDGE, :] = jnp.zeros((EDGE, width), f32)
    dext[EDGE + rows :, :] = jnp.zeros((dext.shape[0] - EDGE - rows, width), f32)
    own = w_ref[KW - 1 : KW, :] * dext[EDGE : EDGE + rows, :]
    at = EDGE - (EDGE - KW + 1)
    spill = w_ref[KW - 1 : KW, :] * dext[0:EDGE, :]
    for tap in range(KW):
        back = KW - 1 - tap
        if back:
            own = own + w_ref[tap : tap + 1, :] * dext[EDGE + back : EDGE + back + rows, :]
            spill = spill + w_ref[tap : tap + 1, :] * dext[back : back + EDGE, :]
    own_ref[...] = own.astype(bf16)
    last_ref[...] = own[rows - last_ref.shape[0] :, :]
    spill_ref[...] = spill
    d_conv = dext[EDGE : EDGE + rows, :]
    for tap in range(KW):
        at = EDGE - (KW - 1) + tap
        gw_ref[tap : tap + 1, :] = jnp.sum(d_conv * ext[at : at + rows, :], axis=0, keepdims=True)
    lanes = lax.broadcasted_iota(jnp.int32, (rows, 8), 1)
    packed = jnp.zeros((rows, 8), f32)
    for h in range(heads):
        packed = jnp.where(lanes == h, col_terms[h][0], packed)
        packed = jnp.where(lanes == heads + h, col_terms[h][1], packed)
    packed = packed.T
    glogit_ref[...] = packed[heads : 2 * heads] * b_row * (1.0 - b_row)
    d_cum = packed[:heads] - jnp.concatenate(row_terms, axis=0)
    onward = jnp.where(i >= j, 1.0, 0.0).astype(bf16)
    d1 = d_cum.astype(bf16)
    rest = d_cum - d1.astype(f32)
    d2 = rest.astype(bf16)
    d3 = (rest - d2.astype(f32)).astype(bf16)
    gdecay_ref[...] = (dot(d3, onward, 1, 0) + dot(d2, onward, 1, 0)) + dot(d1, onward, 1, 0)


def shape_of(*extent, dtype=f32):
    return jax.ShapeDtypeStruct(extent, dtype)


def prepare(x, edge, w, logits, g, do):
    rows, width = x.shape
    heads = g.shape[0]
    return pl.pallas_call(
        prepare_kernel,
        out_shape=(
            shape_of(heads, 3, DK, DK),
            shape_of(heads, rows, rows),
            shape_of(heads, rows, DV),
            shape_of(heads, rows, DK),
            shape_of(heads, rows, rows),
            shape_of(heads, rows, rows),
        ),
        scratch_shapes=[pltpu.VMEM((EDGE + rows, width), f32)],
        compiler_params=pltpu.CompilerParams(vmem_limit_bytes=48 << 20),
        name="prepare",
    )(x, edge, w, logits, g, do)


def backward(slab, x, edge, w, logits, g, do, solve, base, weights, score, gram, state):
    rows, width = x.shape
    heads = g.shape[0]
    return pl.pallas_call(
        backward_kernel,
        out_shape=(
            shape_of(rows, width, dtype=bf16),
            shape_of(slab, width),
            shape_of(EDGE, width),
            shape_of(KW, width),
            shape_of(heads, rows),
            shape_of(heads, rows),
        ),
        scratch_shapes=[
            pltpu.VMEM((EDGE + rows, width), f32),
            pltpu.VMEM((2 * EDGE + rows, width), f32),
        ],
        compiler_params=pltpu.CompilerParams(vmem_limit_bytes=48 << 20),
        name="backward",
    )(x, edge, w, logits, g, do, solve, base, weights, score, gram, state)


def ctx_at(i):
    return {"ctx": i}


def head_at(i):
    return {"head": i}


def remote(src, dst, send, recv, device):
    return pltpu.make_async_remote_copy(
        src_ref=src,
        dst_ref=dst,
        send_sem=send,
        recv_sem=recv,
        device_id=device,
        device_id_type=pl.DeviceIdType.MESH,
    )


def greet(devices):
    barrier = pltpu.get_barrier_semaphore()
    for device in devices:
        pl.semaphore_signal(
            barrier, inc=1, device_id=device, device_id_type=pl.DeviceIdType.MESH
        )
    pl.semaphore_wait(barrier, len(devices))


def far_first(n):
    order = []
    for d in range(n // 2, 0, -1):
        order += [d] if 2 * d == n else [d, n - d]
    return order


def gather_kernel(n, nc, x_ref, out_ref, edge_ref, send, recv, edge_send, edge_recv, own_sem):
    me, c = lax.axis_index("head"), lax.axis_index("ctx")
    slab, width = x_ref.shape[0], out_ref.shape[1]
    rows = out_ref.shape[0]

    def slab_at(z):
        return out_ref.at[pl.ds(pl.multiple_of(z * slab, slab), slab), :]

    def cols(z):
        return x_ref.at[:, pl.ds(pl.multiple_of(z * width, width), width)]

    after, before = lax.rem(c + 1, nc), lax.rem(c + nc - 1, nc)
    greet([head_at(lax.rem(me + d, n)) for d in range(1, n)] + [ctx_at(after), ctx_at(before)])
    own = pltpu.make_async_copy(cols(me), slab_at(me), own_sem)
    own.start()

    def copy(d):
        to = lax.rem(me + d, n)
        return remote(cols(to), slab_at(me), send.at[d], recv.at[d], head_at(to))

    def arriving(d):
        source = lax.rem(me + n - d, n)
        return remote(cols(me), slab_at(source), send.at[d], recv.at[d], head_at(source))

    for d in far_first(n):
        copy(d).start()
    last = lax.rem(me + 1, n)

    @pl.when(last != 0)
    def _():
        arriving(last).wait_recv()

    @pl.when(last == 0)
    def _():
        own.wait()

    edge = remote(
        out_ref.at[pl.ds(rows - EDGE, EDGE), :], edge_ref, edge_send, edge_recv, ctx_at(after)
    )
    edge.start()

    @pl.when(last != 0)
    def _():
        own.wait()

    for d in range(1, n):

        @pl.when(last != d)
        def _():
            arriving(d).wait_recv()

    for d in range(1, n):
        copy(d).wait_send()
    edge.wait()


def gather_tokens(x):
    n, nc = lax.axis_size("head"), lax.axis_size("ctx")
    slab, width = x.shape
    return pl.pallas_call(
        functools.partial(gather_kernel, n, nc),
        out_shape=(
            shape_of(slab * n, width // n, dtype=bf16),
            shape_of(EDGE, width // n, dtype=bf16),
        ),
        in_specs=[pl.BlockSpec(memory_space=pl.ANY)],
        out_specs=(pl.BlockSpec(memory_space=pl.ANY), pl.BlockSpec(memory_space=pl.ANY)),
        scratch_shapes=[
            pltpu.SemaphoreType.DMA((n,)),
            pltpu.SemaphoreType.DMA((n,)),
            pltpu.SemaphoreType.DMA,
            pltpu.SemaphoreType.DMA,
            pltpu.SemaphoreType.DMA,
        ],
        compiler_params=pltpu.CompilerParams(collective_id=1, has_side_effects=True),
        name="gather_tokens",
    )(x)


def scan_kernel(
    chips, maps_ref, first_ref, final_ref, state_ref,
    sib, start, end, every, cut_out, cut_in, s_out, d_out, s_in, d_in, give,
    sib_sem, a_send, a_recv, cut_send, cut_recv, s_send, s_recv, d_send, d_recv, give_sem,
):
    c = lax.axis_index("ctx")
    q, k = lax.div(c, 2), lax.rem(c, 2)
    share = DV // chips
    sibling = ctx_at(c + 1 - 2 * k)

    def chip(p):
        return ctx_at(2 * p + k)

    others = [lax.rem(q + d, chips) for d in range(1, chips)]
    greet([chip(p) for p in others] + [sibling])
    swap = remote(maps_ref.at[1 - k], sib, sib_sem.at[0], sib_sem.at[1], sibling)
    swap.start()
    start[...] = first_ref[k].T
    end[...] = final_ref[k].T
    swap.wait_recv()
    low = k == 0
    mine = maps_ref[k]
    theirs = sib[...]
    a1, b1, c1 = [jnp.where(low, mine[i], theirs[i]) for i in range(3)]
    a2, b2, c2 = [jnp.where(low, theirs[i], mine[i]) for i in range(3)]
    a1, a2 = split(a1), split(a2)
    every[q] = mm(a1, a2)
    b12 = mm(split(b1), a2) + b2
    c12 = mm(split(c2), a1, 1, 1) + c1
    cut_out[:, :share, :] = b12.reshape(chips, share, DK)
    cut_out[:, share:, :] = c12.reshape(chips, share, DK)
    order = far_first(chips)

    def a_copy(d):
        to = lax.rem(q + d, chips)
        return remote(every.at[q], every.at[q], a_send.at[d], a_recv.at[q], chip(to))

    def cut_copy(d):
        to = lax.rem(q + d, chips)
        return remote(cut_out.at[to], cut_in.at[q], cut_send.at[d], cut_recv.at[q], chip(to))

    for d in order:
        cut_copy(d).start()
        a_copy(d).start()
    cut_in[q] = cut_out[q]
    my_rows = pl.ds(pl.multiple_of(q * share, share), share)
    s, d = start[my_rows, :], end[my_rows, :]
    here = set()

    def arrive(p):
        if p in here:
            return
        here.add(p)

        @pl.when(q != p)
        def _():
            remote(every.at[q], every.at[p], a_send.at[0], a_recv.at[p], chip(p)).wait_recv()
            remote(cut_out.at[p], cut_in.at[p], cut_send.at[0], cut_recv.at[p], chip(p)).wait_recv()

    def hand_out(p, value, out, into, send, recv):
        out[p] = value

        @pl.when(q != p)
        def _():
            remote(out.at[p], into.at[my_rows, :], send.at[p], recv.at[q], chip(p)).start()

        @pl.when(q == p)
        def _():
            into[my_rows, :] = value

    for t in range(chips):
        u = chips - 1 - t
        hand_out(t, s, s_out, s_in, s_send, s_recv)
        hand_out(u, d, d_out, d_in, d_send, d_recv)
        if t < chips - 1:
            arrive(t)
            arrive(u)
            s = mm(split(s), split(every[t])) + cut_in[t, :share, :]
            d = mm(split(d), split(every[u]), 1, 1) + cut_in[u, share:, :]

    def finish(p, out, into, send, recv):
        rows = pl.ds(p * share, share)

        @pl.when(q != p)
        def _():
            copy = remote(out.at[p], into.at[rows, :], send.at[p], recv.at[p], chip(p))
            copy.wait_recv()
            copy.wait_send()

    for p in range(chips):
        finish(p, s_out, s_in, s_send, s_recv)
        finish(p, d_out, d_in, d_send, d_recv)
    s, d = s_in[...], d_in[...]
    s2 = mm(split(s), a1) + b1
    d1 = mm(split(d), a2, 1, 1) + c2
    give[0] = jnp.where(low, s2, s)
    give[1] = jnp.where(low, d, d1)
    pass_on = remote(give, state_ref.at[k], give_sem.at[0], give_sem.at[1], sibling)
    pass_on.start()
    state_ref[k, 0] = jnp.where(low, s, s2)
    state_ref[k, 1] = jnp.where(low, d1, d)
    swap.wait_send()
    for d in range(1, chips):
        a_copy(d).wait_send()
        cut_copy(d).wait_send()
    pass_on.wait()


def scan_states(maps, initial_state, final_state_grad):
    chips = lax.axis_size("ctx") // 2
    heads = maps.shape[0]
    share = DV // chips
    sems = pltpu.SemaphoreType.DMA
    whole = pl.BlockSpec(memory_space=pltpu.VMEM)
    return pl.pallas_call(
        functools.partial(scan_kernel, chips),
        out_shape=shape_of(heads, 2, DV, DK),
        in_specs=[whole] * 3,
        out_specs=whole,
        scratch_shapes=[
            pltpu.VMEM((3, DK, DK), f32),
            pltpu.VMEM((DV, DK), f32),
            pltpu.VMEM((DV, DK), f32),
            pltpu.VMEM((chips, DK, DK), f32),
            pltpu.VMEM((chips, 2 * share, DK), f32),
            pltpu.VMEM((chips, 2 * share, DK), f32),
            pltpu.VMEM((chips, share, DK), f32),
            pltpu.VMEM((chips, share, DK), f32),
            pltpu.VMEM((DV, DK), f32),
            pltpu.VMEM((DV, DK), f32),
            pltpu.VMEM((2, DV, DK), f32),
            sems((2,)),
            sems((chips,)),
            sems((chips,)),
            sems((chips,)),
            sems((chips,)),
            sems((chips,)),
            sems((chips,)),
            sems((chips,)),
            sems((chips,)),
            sems((2,)),
        ],
        compiler_params=pltpu.CompilerParams(collective_id=2, has_side_effects=True),
        name="scan_states",
    )(maps, initial_state, final_state_grad)


def return_kernel(
    n, nc, near, own_ref, last_ref, spill_ref, gw_ref, out_ref, total_ref,
    final, inbox, near_sums, far_sums,
    send, recv, own_sem, spill_sem, near_send, near_recv, far_send, far_recv,
):
    me, c = lax.axis_index("head"), lax.axis_index("ctx")
    slab = out_ref.shape[0]
    width = own_ref.shape[1]
    g, r = lax.div(c, near), lax.rem(c, near)
    far = nc // near
    after, before = lax.rem(c + 1, nc), lax.rem(c + nc - 1, nc)

    def near_at(d):
        return ctx_at(g * near + lax.rem(r + d, near))

    def far_at(d):
        return ctx_at(lax.rem(g + d, far) * near + r)

    greet(
        [head_at(lax.rem(me + d, n)) for d in range(1, n)]
        + [ctx_at(after), ctx_at(before)]
        + [near_at(d) for d in range(1, near)]
        + [far_at(d) for d in range(1, far)]
    )
    spilled = remote(spill_ref, inbox, spill_sem.at[0], spill_sem.at[1], ctx_at(before))
    spilled.start()
    near_sums[r] = gw_ref[...]

    def near_copy(d):
        return remote(near_sums.at[r], near_sums.at[r], near_send.at[d], near_recv.at[r], near_at(d))

    def far_copy(d):
        return remote(far_sums.at[g], far_sums.at[g], far_send.at[d], far_recv.at[g], far_at(d))

    for d in range(1, near):
        near_copy(d).start()

    def slab_at(z):
        return own_ref.at[pl.ds(pl.multiple_of(z * slab, slab), slab), :]

    def cols(z):
        return out_ref.at[:, pl.ds(pl.multiple_of(z * width, width), width)]

    def copy(d, source=None):
        to = lax.rem(me + d, n)
        source = slab_at(to) if source is None else source
        return remote(source, cols(me), send.at[d], recv.at[d], head_at(to))

    for d in far_first(n):

        @pl.when(lax.rem(me + d, n) != n - 1)
        def _():
            copy(d).start()

    own = pltpu.make_async_copy(slab_at(me), cols(me), own_sem)
    own_last = pltpu.make_async_copy(final, cols(me), own_sem)

    @pl.when(me != n - 1)
    def _():
        own.start()

    spilled.wait()
    final[...] = last_ref[...].astype(bf16)
    more = jnp.where(c < nc - 1, inbox[...], 0.0)
    final[slab - EDGE :, :] = (last_ref[slab - EDGE :, :] + more).astype(bf16)
    last = lax.rem(2 * n - 1 - me, n)

    @pl.when(me != n - 1)
    def _():
        copy(last, final).start()

    @pl.when(me == n - 1)
    def _():
        own_last.start()

    for d in range(1, near):
        source = lax.rem(r + near - d, near)
        remote(
            near_sums.at[r], near_sums.at[source], near_send.at[d], near_recv.at[source], near_at(d)
        ).wait_recv()
    total = near_sums[0]
    for i in range(1, near):
        total = total + near_sums[i]
    far_sums[g] = total
    for d in range(1, far):
        far_copy(d).start()
    for d in range(1, far):
        source = lax.rem(g + far - d, far)
        remote(
            far_sums.at[g], far_sums.at[source], far_send.at[d], far_recv.at[source], far_at(d)
        ).wait_recv()
    total = far_sums[0]
    for i in range(1, far):
        total = total + far_sums[i]
    total_ref[...] = total
    for d in range(1, near):
        near_copy(d).wait_send()
    for d in range(1, far):
        far_copy(d).wait_send()
    for d in range(1, n):
        source = lax.rem(me + n - d, n)
        remote(slab_at(me), cols(source), send.at[d], recv.at[d], head_at(source)).wait_recv()
        copy(d, final).wait_send()
    own_last.wait()


def return_tokens(own, last, spill, gw):
    n, nc = lax.axis_size("head"), lax.axis_size("ctx")
    near = 8
    rows, width = own.shape
    sems = pltpu.SemaphoreType.DMA
    whole = pl.BlockSpec(memory_space=pltpu.VMEM)
    anywhere = pl.BlockSpec(memory_space=pl.ANY)
    return pl.pallas_call(
        functools.partial(return_kernel, n, nc, near),
        out_shape=(shape_of(rows // n, width * n, dtype=bf16), shape_of(*gw.shape)),
        in_specs=[anywhere, whole, whole, whole],
        out_specs=(anywhere, whole),
        scratch_shapes=[
            pltpu.VMEM((rows // n, width), bf16),
            pltpu.VMEM(spill.shape, f32),
            pltpu.VMEM((near, *gw.shape), f32),
            pltpu.VMEM((nc // near, *gw.shape), f32),
            sems((n,)),
            sems((n,)),
            sems,
            sems((2,)),
            sems((near,)),
            sems((near,)),
            sems((nc // near,)),
            sems((nc // near,)),
        ],
        compiler_params=pltpu.CompilerParams(collective_id=3, has_side_effects=True),
        name="return_tokens",
    )(own, last, spill, gw)


def on_device(mixed_in, conv_weight, logits, decay_log, initial_state, final_state_grad, grad_out):
    x, edge = gather_tokens(mixed_in)
    maps, *kept = prepare(x, edge, conv_weight, logits, decay_log, grad_out)
    state = scan_states(maps, initial_state, final_state_grad)
    own, last, spill, gw, glogit, gdecay = backward(
        mixed_in.shape[0], x, edge, conv_weight, logits, decay_log, grad_out, *kept, state
    )
    returned, total = return_tokens(own, last, spill, gw)
    return (returned, total, glogit, gdecay)


def solution(mesh):
    in_specs = (
        P(("ctx", "head"), None),
        P(None, "head"),
        P("head", "ctx"),
        P("head", "ctx"),
        P("head", None, None),
        P("head", None, None),
        P("ctx", "head"),
    )
    out_specs = (P(("ctx", "head"), None), P(None, "head"), P("head", "ctx"), P("head", "ctx"))
    return jax.shard_map(
        on_device, mesh=mesh, in_specs=in_specs, out_specs=out_specs, check_vma=False
    )
```

```python
import functools
import jax
import jax.numpy as jnp
from jax import lax
from jax.experimental import pallas as pl
from jax.experimental.pallas import tpu as pltpu
from jax.sharding import PartitionSpec as P

DK = 128
DV = 128
KW = 4
EDGE = 16

f32 = jnp.float32
bf16 = jnp.bfloat16
norm_eps = 1e-06


def split(a):
    hi = a.astype(bf16)
    return (hi, (a - hi.astype(f32)).astype(bf16))


def dot(a, b, ca, cb):
    return lax.dot_general(a, b, (((ca,), (cb,)), ((), ())), preferred_element_type=f32)


def mm(a, b, ca=1, cb=0):
    out = dot(a[0], b[0], ca, cb)
    if len(b) > 1:
        out = out + dot(a[0], b[1], ca, cb)
    if len(a) > 1:
        out = out + dot(a[1], b[0], ca, cb)
    return out


def inv_norm(a):
    return lax.rsqrt(jnp.sum(a * a, axis=-1, keepdims=True) + norm_eps)


def gates(logit_ref, g_ref):
    heads, rows = g_ref.shape
    i = lax.broadcasted_iota(jnp.int32, (rows, rows), 0)
    j = lax.broadcasted_iota(jnp.int32, (rows, rows), 1)
    upto = jnp.where(i <= j, 1.0, 0.0).astype(bf16)
    g = g_ref[...]
    g1 = g.astype(bf16)
    rest = g - g1.astype(f32)
    g2 = rest.astype(bf16)
    g3 = (rest - g2.astype(f32)).astype(bf16)
    c_row = (dot(g3, upto, 1, 0) + dot(g2, upto, 1, 0)) + dot(g1, upto, 1, 0)
    b_row = 1.0 / (1.0 + jnp.exp(-logit_ref[...]))
    pad = jnp.zeros((8 - 2 * heads, rows), f32)
    cols = jnp.concatenate([c_row, b_row, pad], axis=0).T
    return c_row, b_row, cols, i, j


def ratios_of(c_col, c_row, i, j):
    return jnp.where(j <= i, jnp.exp(jnp.where(j <= i, c_col - c_row, 0.0)), 0.0)


def invert_unit_lower(low, n):
    i = lax.broadcasted_iota(jnp.int32, (n, n), 0)
    j = lax.broadcasted_iota(jnp.int32, (n, n), 1)
    eye = jnp.where(i == j, 1.0, 0.0)
    inv = [eye - jnp.where((i ^ j) == 1, part, 0.0) for part in low]
    shift = 1
    while (1 << shift) < n:
        pick = ((i >> shift) ^ (j >> shift)) == 1
        parts = [split(a) for a in inv]
        mid = [
            mm(p, split(jnp.where(pick, part, 0.0))) for p, part in zip(parts, low)
        ]
        inv = [a - mm(split(m), p) for a, m, p in zip(inv, mid, parts)]
        shift += 1
    return inv


def shape_of(*extent, dtype=f32):
    return jax.ShapeDtypeStruct(extent, dtype)


def ctx_at(i):
    return {"ctx": i}


def head_at(i):
    return {"head": i}


def remote(src, dst, send, recv, device):
    return pltpu.make_async_remote_copy(
        src_ref=src,
        dst_ref=dst,
        send_sem=send,
        recv_sem=recv,
        device_id=device,
        device_id_type=pl.DeviceIdType.MESH,
    )


def greet(devices):
    barrier = pltpu.get_barrier_semaphore()
    for device in devices:
        pl.semaphore_signal(
            barrier, inc=1, device_id=device, device_id_type=pl.DeviceIdType.MESH
        )
    pl.semaphore_wait(barrier, len(devices))


def far_first(n):
    order = []
    for d in range(n // 2, 0, -1):
        order += [d] if 2 * d == n else [d, n - d]
    return order


def layer_kernel(
    n, nc, x_hbm, w_hbm, logit_hbm, g_hbm, do_hbm, first_hbm, final_hbm,
    out_hbm, total_hbm, glogit_hbm, gdecay_hbm,
    w_ref, logit_ref, g_ref, do_ref, start, end,
    x_in, edge, ext, dext, conv_ref, sig_ref, qk_ref,
    ratio_ref, gram_ref, score_ref, solve_ref, base_ref, weight_ref, push_ref,
    a_mine, bc_mine, a_sib, bc_sib, every, cut_out, cut_in,
    s_out, d_out, s_in, d_in, give, state_ref,
    own_ref, tail_ref, spill_ref, inbox, last_ref,
    gw_ref, gw_sib, gw_all, total_ref, glogit_ref, gdecay_ref,
    load_sem, store_sem, own_sem, x_send, x_recv, edge_send, edge_recv, swap_send, swap_recv,
    a_send, a_recv, cut_send, cut_recv, s_send, s_recv, d_send, d_recv,
    spill_send, spill_recv, back_send, back_recv, gw_send, gw_recv,
):
    me, c = lax.axis_index("head"), lax.axis_index("ctx")
    heads, rows = g_ref.shape
    slab, width = x_hbm.shape[0], x_in.shape[1]
    half = rows // 2
    chips = nc // 2
    share = DV // chips
    q_at, k_at = lax.div(c, 2), lax.rem(c, 2)
    low = k_at == 0
    after, before = lax.rem(c + 1, nc), lax.rem(c + nc - 1, nc)
    sibling = ctx_at(c + 1 - 2 * k_at)
    other = ctx_at(lax.rem(c + nc - 1 + 2 * k_at, nc))

    def chip(p):
        return ctx_at(2 * p + k_at)

    def chip_off(d):
        return lax.rem(q_at + d, chips)

    loads = [
        pltpu.make_async_copy(source, target, load_sem.at[i])
        for i, (source, target) in enumerate(
            (
                (logit_hbm, logit_ref),
                (g_hbm, g_ref),
                (w_hbm, w_ref),
                (do_hbm, do_ref),
                (first_hbm.at[k_at], start),
                (final_hbm.at[k_at], end),
            )
        )
    ]
    for load in loads:
        load.start()

    def slab_at(z):
        return x_in.at[pl.ds(pl.multiple_of(z * slab, slab), slab), :]

    def cols(z, at=0, size=width):
        return pl.ds(pl.multiple_of(z * width + at, 128), size)

    own = pltpu.make_async_copy(x_hbm.at[:, cols(me)], slab_at(me), own_sem)
    own.start()
    greet(
        [head_at(lax.rem(me + d, n)) for d in far_first(n)]
        + [chip(chip_off(d)) for d in far_first(chips)]
        + [sibling, other]
    )

    parts = ((DK, DK), (0, DK), (2 * DK, heads * DV))

    def send_x(i, d):
        at, size = parts[i]
        to = lax.rem(me + d, n)
        return remote(
            x_hbm.at[:, cols(to, at, size)],
            slab_at(me).at[:, pl.ds(at, size)],
            x_send.at[i, d], x_recv.at[i, d], head_at(to),
        )

    def take_x(i, d):
        at, size = parts[i]
        source = lax.rem(me + n - d, n)
        remote(
            x_hbm.at[:, cols(me, at, size)],
            slab_at(source).at[:, pl.ds(at, size)],
            x_send.at[i, d], x_recv.at[i, d], head_at(source),
        ).wait_recv()

    for i in range(3):
        for d in far_first(n):
            send_x(i, d).start()

    def send_edge(i):
        at, size = parts[i]
        return remote(
            x_in.at[pl.ds(rows - EDGE, EDGE), pl.ds(at, size)],
            edge.at[:, pl.ds(at, size)],
            edge_send.at[i], edge_recv.at[i], ctx_at(after),
        )

    for load in loads[:3]:
        load.wait()
    c_row, b_row, wide_cols, i, j = gates(logit_ref, g_ref)

    def col(h):
        return wide_cols[:, h : h + 1]

    def beta(h):
        return wide_cols[:, heads + h : heads + h + 1]

    for h in range(heads):
        ratio_ref[h] = ratios_of(col(h), c_row[h : h + 1, :], i, j)
    last_from = lax.rem(me + 1, n)
    own.wait()

    def convolve(i):
        at, size = parts[i]

        @pl.when(last_from != 0)
        def _():
            take_x(i, last_from)

        send_edge(i).start()
        for d in range(n - 1, 0, -1):

            @pl.when(last_from != d)
            def _():
                take_x(i, d)

        send_edge(i).wait_recv()
        span = slice(at, at + size)
        ext[0:EDGE, span] = jnp.where(c > 0, edge[:, span].astype(f32), 0.0)
        ext[EDGE : EDGE + rows, span] = x_in[:, span].astype(f32)
        conv = w_ref[KW - 1 : KW, span] * ext[EDGE : EDGE + rows, span]
        for tap in range(KW - 1):
            row = EDGE - (KW - 1) + tap
            conv = conv + w_ref[tap : tap + 1, span] * ext[row : row + rows, span]
        sig = 1.0 / (1.0 + jnp.exp(-conv))
        conv_ref[:, span] = conv
        sig_ref[:, span] = sig
        return conv * sig

    b = convolve(0)
    k = b * inv_norm(b)
    qk_ref[:, DK:] = k
    ks = split(k)
    gram = mm(ks, ks, 1, 1)
    lows = []
    for h in range(heads):
        rg = jnp.where(j < i, ratio_ref[h] * gram, 0.0)
        gram_ref[h] = rg
        lows.append(beta(h) * rg)
    diag = []
    for part in lows:
        diag += [part[:half, :half], part[half:, half:]]
    diag = invert_unit_lower(diag, half)
    for h in range(heads):
        one, two = split(diag[2 * h]), split(diag[2 * h + 1])
        corner = mm(split(mm(two, split(lows[h][half:, :half]))), one)
        solve_ref[h, :half, :half] = diag[2 * h]
        solve_ref[h, :half, half:] = jnp.zeros((half, half), f32)
        solve_ref[h, half:, :half] = -corner
        solve_ref[h, half:, half:] = diag[2 * h + 1]
    ii = lax.broadcasted_iota(jnp.int32, (DK, DK), 0)
    jj = lax.broadcasted_iota(jnp.int32, (DK, DK), 1)

    def tail_keys(h):
        return jnp.exp(col(h)[rows - 1 : rows, :] - col(h))

    for h in range(heads):
        weights = mm(split(solve_ref[h]), split((beta(h) * jnp.exp(col(h))) * k))
        weight_ref[h] = weights
        total_decay = jnp.exp(col(h)[rows - 1 : rows, :])
        a_mine[h] = jnp.where(ii == jj, total_decay, 0.0) - mm(
            split(weights), split(tail_keys(h) * k), 0, 0
        )
    swap_a = remote(a_mine.at[1 - k_at], a_sib, swap_send.at[0], swap_recv.at[0], sibling)
    swap_a.start()
    swap_a.wait_recv()
    mine, theirs = a_mine[k_at], a_sib[...]
    a1 = split(jnp.where(low, mine, theirs))
    a2 = split(jnp.where(low, theirs, mine))
    every[q_at] = mm(a1, a2)

    def a_copy(d):
        return remote(
            every.at[q_at], every.at[q_at], a_send.at[d], a_recv.at[q_at], chip(chip_off(d))
        )

    for d in far_first(chips):
        a_copy(d).start()

    a = convolve(1)
    q = a * (inv_norm(a) * DK**-0.5)
    qk_ref[:, :DK] = q
    qk = mm(split(q), ks, 1, 1)
    for load in loads[3:]:
        load.wait()
    for h in range(heads):
        score_ref[h] = ratio_ref[h] * qk
        score = split(score_ref[h])
        do = (do_ref[:, h * DV : (h + 1) * DV],)
        reach = jnp.exp(col(h)) * q - mm(score, split(weight_ref[h]))
        bc_mine[h, 1] = mm(do, split(reach), 0, 0)
        push_ref[h] = mm(score, do, 0, 0)
    values = convolve(2)
    for h in range(heads):
        base = mm(split(solve_ref[h]), split(beta(h) * values[:, h * DV : (h + 1) * DV]))
        base_ref[h] = base
        bc_mine[h, 0] = mm(split(base), split(tail_keys(h) * k), 0, 0)
    swap_bc = remote(bc_mine.at[1 - k_at], bc_sib, swap_send.at[1], swap_recv.at[1], sibling)
    swap_bc.start()
    swap_bc.wait_recv()
    mine, theirs = bc_mine[k_at], bc_sib[...]
    b1, c1 = jnp.where(low, mine[0], theirs[0]), jnp.where(low, mine[1], theirs[1])
    b2, c2 = jnp.where(low, theirs[0], mine[0]), jnp.where(low, theirs[1], mine[1])
    b12 = mm(split(b1), a2) + b2
    c12 = mm(split(c2), a1, 1, 1) + c1
    cut_out[:, :share, :] = b12.reshape(chips, share, DK)
    cut_out[:, share:, :] = c12.reshape(chips, share, DK)

    def cut_copy(d):
        to = chip_off(d)
        return remote(cut_out.at[to], cut_in.at[q_at], cut_send.at[d], cut_recv.at[q_at], chip(to))

    for d in far_first(chips):
        cut_copy(d).start()
    cut_in[q_at] = cut_out[q_at]
    start[...] = start[...].T
    end[...] = end[...].T
    my_rows = pl.ds(pl.multiple_of(q_at * share, share), share)
    s, d = start[my_rows, :], end[my_rows, :]
    here = set()

    def arrive(p):
        if p in here:
            return
        here.add(p)

        @pl.when(q_at != p)
        def _():
            remote(every.at[p], every.at[p], a_send.at[0], a_recv.at[p], chip(p)).wait_recv()
            remote(cut_out.at[p], cut_in.at[p], cut_send.at[0], cut_recv.at[p], chip(p)).wait_recv()

    def hand_out(p, value, out, into, send, recv):
        out[p] = value

        @pl.when(q_at != p)
        def _():
            remote(out.at[p], into.at[my_rows, :], send.at[p], recv.at[q_at], chip(p)).start()

        @pl.when(q_at == p)
        def _():
            into[my_rows, :] = value

    for t in range(chips):
        u = chips - 1 - t
        hand_out(t, s, s_out, s_in, s_send, s_recv)
        hand_out(u, d, d_out, d_in, d_send, d_recv)
        if t < chips - 1:
            arrive(t)
            arrive(u)
            s = mm(split(s), split(every[t])) + cut_in[t, :share, :]
            d = mm(split(d), split(every[u]), 1, 1) + cut_in[u, share:, :]

    def tile(p, out, into, send, recv):
        return remote(
            out.at[p], into.at[pl.ds(p * share, share), :], send.at[p], recv.at[p], chip(p)
        )

    for p in range(chips):

        @pl.when(q_at != p)
        def _():
            tile(p, s_out, s_in, s_send, s_recv).wait_recv()
            tile(p, d_out, d_in, d_send, d_recv).wait_recv()

    s, d = s_in[...], d_in[...]
    s2 = mm(split(s), a1) + b1
    d1 = mm(split(d), a2, 1, 1) + c2
    give[0] = jnp.where(low, s2, s)
    give[1] = jnp.where(low, d, d1)
    pass_on = remote(give, state_ref.at[k_at], swap_send.at[2], swap_recv.at[2], sibling)
    pass_on.start()
    state_ref[k_at, 0] = jnp.where(low, s, s2)
    state_ref[k_at, 1] = jnp.where(low, d1, d)
    pass_on.wait_recv()

    dext[0:EDGE, :] = jnp.zeros((EDGE, width), f32)
    dext[EDGE + rows :, :] = jnp.zeros((dext.shape[0] - EDGE - rows, width), f32)

    def silu_slope(span):
        s = sig_ref[:, span]
        return s * (1.0 + conv_ref[:, span] * (1.0 - s))

    spans = ((2 * DK, heads * DV), (0, 2 * DK))

    def spill_copy(i):
        at, size = spans[i]
        span = pl.ds(at, size)
        return remote(
            spill_ref.at[:, span], inbox.at[:, span],
            spill_send.at[i], spill_recv.at[i], ctx_at(before),
        )

    def send_back(i, d, source=None):
        at, size = spans[i]
        to = lax.rem(me + d, n)
        if source is None:
            source = own_ref.at[pl.ds(pl.multiple_of(to * slab, slab), slab), :]
        return remote(
            source.at[:, pl.ds(at, size)], out_hbm.at[:, cols(me, at, size)],
            back_send.at[i, d], back_recv.at[i, d], head_at(to),
        )

    def unconvolve(i):
        at, size = spans[i]
        span = slice(at, at + size)
        own = w_ref[KW - 1 : KW, span] * dext[EDGE : EDGE + rows, span]
        spill = w_ref[KW - 1 : KW, span] * dext[0:EDGE, span]
        for tap in range(KW - 1):
            back = KW - 1 - tap
            own = own + w_ref[tap : tap + 1, span] * dext[EDGE + back : EDGE + back + rows, span]
            spill = spill + w_ref[tap : tap + 1, span] * dext[back : back + EDGE, span]
        spill_ref[:, span] = spill
        spill_copy(i).start()
        own_ref[:, span] = own.astype(bf16)
        tail_ref[:, span] = own[rows - slab :, :]
        for d in far_first(n):

            @pl.when(lax.rem(me + d, n) != n - 1)
            def _():
                send_back(i, d).start()

    q, k = qk_ref[:, :DK], qk_ref[:, DK:]
    qs, ks = split(q), split(k)
    lower = j < i
    kept = []
    for h in range(heads):
        sts, dsts = split(state_ref[h, 0]), split(state_ref[h, 1])
        tail_k = tail_keys(h) * k
        update = base_ref[h] - mm(split(weight_ref[h]), sts, 1, 1)
        d_update = push_ref[h] + mm(split(tail_k), dsts, 1, 1)
        x = mm(split(solve_ref[h]), split(d_update), 0, 0)
        span = slice(2 * DK + h * DV, 2 * DK + (h + 1) * DV)
        dext[EDGE : EDGE + rows, span] = (beta(h) * x) * silu_slope(span)
        v = conv_ref[:, span] * sig_ref[:, span]
        kept.append((sts, dsts, tail_k, split(update), split(x), jnp.sum(x * v, axis=1, keepdims=True)))
    unconvolve(0)
    dq = None
    row_terms, col_terms = [], []
    for h in range(heads):
        sts, dsts, tail_k, us, xs, xv = kept[h]
        decays = jnp.exp(col(h))
        total_decay = jnp.exp(col(h)[rows - 1 : rows, :])
        ratios = ratio_ref[h]
        score = score_ref[h]
        do = (do_ref[:, h * DV : (h + 1) * DV],)
        d_score = mm(do, us, 1, 1)
        d_low = -mm(xs, us, 1, 1)
        y = -mm(xs, sts)
        d_tail = mm(us, dsts)
        rgd = gram_ref[h] * d_low
        part_q = decays * mm(do, sts)
        part_k = tail_keys(h) * d_tail + (beta(h) * decays) * y
        z = ratios * d_score
        d_gram = jnp.where(lower, beta(h) * (ratios * d_low), 0.0)
        if dq is None:
            dq, dk, zs, dgs = part_q, part_k, z, d_gram
        else:
            dq, dk, zs, dgs = dq + part_q, dk + part_k, zs + z, dgs + d_gram
        flow = jnp.where(lower, score * d_score, 0.0) + beta(h) * rgd
        yk = decays * jnp.sum(y * k, axis=1, keepdims=True)
        tk = jnp.sum(tail_k * d_tail, axis=1, keepdims=True)
        d_beta = xv + yk + jnp.sum(rgd, axis=1, keepdims=True)
        d_cum = (
            jnp.sum(flow, axis=1, keepdims=True)
            + jnp.sum(q * part_q, axis=1, keepdims=True)
            + beta(h) * yk
            - tk
        )
        ends = total_decay * jnp.sum(
            state_ref[h, 0] * state_ref[h, 1], keepdims=True
        ) + jnp.sum(tk, keepdims=True)
        at_end = lax.broadcasted_iota(jnp.int32, (rows, 1), 0) == rows - 1
        col_terms.append((d_cum + jnp.where(at_end, ends, 0.0), d_beta))
        row_terms.append(jnp.sum(flow, axis=0, keepdims=True))
    zs, dgs = split(zs), split(dgs)
    dq = dq + mm(zs, ks)
    dk = dk + mm(zs, qs, 0, 0) + mm(dgs, ks) + mm(dgs, ks, 0, 0)
    for at, d, factor in ((0, dq, DK**-0.5), (DK, dk, 1.0)):
        span = slice(at, at + DK)
        value = conv_ref[:, span] * sig_ref[:, span]
        inv = inv_norm(value)
        inner = jnp.sum(value * d, axis=1, keepdims=True)
        d_act = (inv * factor) * (d - value * (inv * inv * inner))
        dext[EDGE : EDGE + rows, span] = d_act * silu_slope(span)
    unconvolve(1)
    d_conv = dext[EDGE : EDGE + rows, :]
    for tap in range(KW):
        row = EDGE - (KW - 1) + tap
        gw_ref[tap : tap + 1, :] = jnp.sum(d_conv * ext[row : row + rows, :], axis=0, keepdims=True)
    swap_gw = remote(gw_ref, gw_sib, swap_send.at[3], swap_recv.at[3], sibling)
    swap_gw.start()

    for i_part in range(2):
        spill_copy(i_part).wait_recv()
    last_ref[...] = tail_ref[...].astype(bf16)
    more = jnp.where(c < nc - 1, inbox[...], 0.0)
    last_ref[slab - EDGE :, :] = (tail_ref[slab - EDGE :, :] + more).astype(bf16)
    to_last = lax.rem(2 * n - 1 - me, n)
    mine_out = out_hbm.at[:, cols(me)]
    own_back = pltpu.make_async_copy(
        own_ref.at[pl.ds(pl.multiple_of(me * slab, slab), slab), :], mine_out, own_sem
    )
    last_back = pltpu.make_async_copy(last_ref, mine_out, own_sem)

    @pl.when(me != n - 1)
    def _():
        for i_part in range(2):
            send_back(i_part, to_last, last_ref).start()
        own_back.start()

    @pl.when(me == n - 1)
    def _():
        last_back.start()

    swap_gw.wait_recv()
    gw_all[q_at] = jnp.where(low, gw_ref[...], gw_sib[...]) + jnp.where(low, gw_sib[...], gw_ref[...])

    def gw_copy(d):
        return remote(
            gw_all.at[q_at], gw_all.at[q_at], gw_send.at[d], gw_recv.at[q_at], chip(chip_off(d))
        )

    for d in far_first(chips):
        gw_copy(d).start()
    lanes = lax.broadcasted_iota(jnp.int32, (rows, 8), 1)
    packed = jnp.zeros((rows, 8), f32)
    for h in range(heads):
        packed = jnp.where(lanes == h, col_terms[h][0], packed)
        packed = jnp.where(lanes == heads + h, col_terms[h][1], packed)
    packed = packed.T
    glogit_ref[...] = packed[heads : 2 * heads] * b_row * (1.0 - b_row)
    d_cum = packed[:heads] - jnp.concatenate(row_terms, axis=0)
    onward = jnp.where(i >= j, 1.0, 0.0).astype(bf16)
    d1 = d_cum.astype(bf16)
    rest = d_cum - d1.astype(f32)
    d2 = rest.astype(bf16)
    d3 = (rest - d2.astype(f32)).astype(bf16)
    gdecay_ref[...] = (dot(d3, onward, 1, 0) + dot(d2, onward, 1, 0)) + dot(d1, onward, 1, 0)
    stores = [
        pltpu.make_async_copy(glogit_ref, glogit_hbm, store_sem.at[0]),
        pltpu.make_async_copy(gdecay_ref, gdecay_hbm, store_sem.at[1]),
        pltpu.make_async_copy(total_ref, total_hbm, store_sem.at[2]),
    ]
    stores[0].start()
    stores[1].start()
    for d in range(1, chips):
        source = chip_off(d)
        remote(
            gw_all.at[q_at], gw_all.at[source], gw_send.at[d], gw_recv.at[source], chip(source)
        ).wait_recv()
    total = gw_all[0]
    for p in range(1, chips):
        total = total + gw_all[p]
    total_ref[...] = total
    stores[2].start()

    for i_part in range(3):
        for d in range(1, n):
            send_x(i_part, d).wait_send()
        send_edge(i_part).wait_send()
    for swap in (swap_a, swap_bc, pass_on, swap_gw):
        swap.wait_send()
    for d in range(1, chips):
        a_copy(d).wait_send()
        cut_copy(d).wait_send()
        gw_copy(d).wait_send()
    for p in range(chips):

        @pl.when(q_at != p)
        def _():
            tile(p, s_out, s_in, s_send, s_recv).wait_send()
            tile(p, d_out, d_in, d_send, d_recv).wait_send()

    for i_part in range(2):
        at, size = spans[i_part]
        spill_copy(i_part).wait_send()
        for d in range(1, n):
            source = lax.rem(me + n - d, n)
            send_back(i_part, d, last_ref).wait_send()
            remote(
                last_ref.at[:, pl.ds(at, size)], out_hbm.at[:, cols(source, at, size)],
                back_send.at[i_part, d], back_recv.at[i_part, d], head_at(source),
            ).wait_recv()
    last_back.wait()
    for store in stores:
        store.wait()


def on_device(mixed_in, conv_weight, logits, decay_log, initial_state, final_state_grad, grad_out):
    n, nc = lax.axis_size("head"), lax.axis_size("ctx")
    heads, rows = decay_log.shape
    slab = mixed_in.shape[0]
    width = mixed_in.shape[1] // n
    chips = nc // 2
    share = DV // chips
    sems = pltpu.SemaphoreType.DMA
    vm = pltpu.VMEM
    anywhere = pl.BlockSpec(memory_space=pltpu.HBM)
    square = vm((heads, rows, rows), f32)
    tall = vm((heads, rows, DK), f32)
    state = vm((DV, DK), f32)
    return pl.pallas_call(
        functools.partial(layer_kernel, n, nc),
        out_shape=(
            shape_of(*mixed_in.shape, dtype=bf16),
            shape_of(*conv_weight.shape),
            shape_of(heads, rows),
            shape_of(heads, rows),
        ),
        in_specs=[anywhere] * 7,
        out_specs=(anywhere,) * 4,
        scratch_shapes=[
            vm((KW, width), f32), vm((heads, rows), f32), vm((heads, rows), f32),
            vm((rows, heads * DV), bf16), state, state,
            vm((rows, width), bf16), vm((EDGE, width), bf16),
            vm((EDGE + rows, width), f32), vm((2 * EDGE + rows, width), f32),
            vm((rows, width), f32), vm((rows, width), f32), vm((rows, 2 * DK), f32),
            square, square, square, square, tall, tall, tall,
            vm((heads, DK, DK), f32), vm((heads, 2, DV, DK), f32), state, vm((2, DV, DK), f32),
            vm((chips, DK, DK), f32),
            vm((chips, 2 * share, DK), f32), vm((chips, 2 * share, DK), f32),
            vm((chips, share, DK), f32), vm((chips, share, DK), f32), state, state,
            vm((2, DV, DK), f32), vm((heads, 2, DV, DK), f32),
            vm((rows, width), bf16), vm((slab, width), f32), vm((EDGE, width), f32),
            vm((EDGE, width), f32), vm((slab, width), bf16),
            vm((KW, width), f32), vm((KW, width), f32), vm((chips, KW, width), f32),
            vm((KW, width), f32), vm((heads, rows), f32), vm((heads, rows), f32),
            sems((6,)), sems((3,)), sems,
            sems((3, n)), sems((3, n)), sems((3,)), sems((3,)), sems((4,)), sems((4,)),
            sems((chips,)), sems((chips,)), sems((chips,)), sems((chips,)),
            sems((chips,)), sems((chips,)), sems((chips,)), sems((chips,)),
            sems((2,)), sems((2,)), sems((2, n)), sems((2, n)), sems((chips,)), sems((chips,)),
        ],
        compiler_params=pltpu.CompilerParams(
            collective_id=1, has_side_effects=True, vmem_limit_bytes=63 << 20
        ),
        name="layer",
    )(mixed_in, conv_weight, logits, decay_log, grad_out, initial_state, final_state_grad)


def solution(mesh):
    in_specs = (
        P(("ctx", "head"), None),
        P(None, "head"),
        P("head", "ctx"),
        P("head", "ctx"),
        P("head", None, None),
        P("head", None, None),
        P("ctx", "head"),
    )
    out_specs = (P(("ctx", "head"), None), P(None, "head"), P("head", "ctx"), P("head", "ctx"))
    return jax.shard_map(
        on_device, mesh=mesh, in_specs=in_specs, out_specs=out_specs, check_vma=False
    )
```

```python
import functools
import jax
import jax.numpy as jnp
from jax import lax
from jax.experimental import pallas as pl
from jax.experimental.pallas import tpu as pltpu
from jax.sharding import PartitionSpec as P

DK = 128
DV = 128
KW = 4
EDGE = 16

f32 = jnp.float32
bf16 = jnp.bfloat16
norm_eps = 1e-06


def split(a):
    hi = a.astype(bf16)
    return (hi, (a - hi.astype(f32)).astype(bf16))


def dot(a, b, ca, cb):
    return lax.dot_general(a, b, (((ca,), (cb,)), ((), ())), preferred_element_type=f32)


def mm(a, b, ca=1, cb=0):
    out = dot(a[0], b[0], ca, cb)
    if len(b) > 1:
        out = out + dot(a[0], b[1], ca, cb)
    if len(a) > 1:
        out = out + dot(a[1], b[0], ca, cb)
    return out


def inv_norm(a):
    return lax.rsqrt(jnp.sum(a * a, axis=-1, keepdims=True) + norm_eps)


def gates(logit_ref, g_ref):
    heads, rows = g_ref.shape
    i = lax.broadcasted_iota(jnp.int32, (rows, rows), 0)
    j = lax.broadcasted_iota(jnp.int32, (rows, rows), 1)
    upto = jnp.where(i <= j, 1.0, 0.0).astype(bf16)
    g = g_ref[...]
    g1 = g.astype(bf16)
    rest = g - g1.astype(f32)
    g2 = rest.astype(bf16)
    g3 = (rest - g2.astype(f32)).astype(bf16)
    c_row = (dot(g3, upto, 1, 0) + dot(g2, upto, 1, 0)) + dot(g1, upto, 1, 0)
    b_row = 1.0 / (1.0 + jnp.exp(-logit_ref[...]))
    pad = jnp.zeros((8 - 2 * heads, rows), f32)
    cols = jnp.concatenate([c_row, b_row, pad], axis=0).T
    return c_row, b_row, cols, i, j


def ratios_of(c_col, c_row, i, j):
    return jnp.where(j <= i, jnp.exp(jnp.where(j <= i, c_col - c_row, 0.0)), 0.0)


def invert_unit_lower(low, n):
    i = lax.broadcasted_iota(jnp.int32, (n, n), 0)
    j = lax.broadcasted_iota(jnp.int32, (n, n), 1)
    eye = jnp.where(i == j, 1.0, 0.0)
    inv = [eye - jnp.where((i ^ j) == 1, part, 0.0) for part in low]
    shift = 1
    while (1 << shift) < n:
        pick = ((i >> shift) ^ (j >> shift)) == 1
        parts = [split(a) for a in inv]
        mid = [
            mm(p, split(jnp.where(pick, part, 0.0))) for p, part in zip(parts, low)
        ]
        inv = [a - mm(split(m), p) for a, m, p in zip(inv, mid, parts)]
        shift += 1
    return inv


def shape_of(*extent, dtype=f32):
    return jax.ShapeDtypeStruct(extent, dtype)


def ctx_at(i):
    return {"ctx": i}


def head_at(i):
    return {"head": i}


def remote(src, dst, send, recv, device):
    return pltpu.make_async_remote_copy(
        src_ref=src,
        dst_ref=dst,
        send_sem=send,
        recv_sem=recv,
        device_id=device,
        device_id_type=pl.DeviceIdType.MESH,
    )


def greet(devices):
    barrier = pltpu.get_barrier_semaphore()
    for device in devices:
        pl.semaphore_signal(
            barrier, inc=1, device_id=device, device_id_type=pl.DeviceIdType.MESH
        )
    pl.semaphore_wait(barrier, len(devices))


def far_first(n):
    order = []
    for d in range(n // 2, 0, -1):
        order += [d] if 2 * d == n else [d, n - d]
    return order


def layer_kernel(
    n, nc, row_len, x_hbm, w_hbm, logit_hbm, g_hbm, do_hbm, first_hbm, final_hbm,
    out_hbm, total_hbm, glogit_hbm, gdecay_hbm,
    w_ref, logit_ref, g_ref, do_ref, start, end,
    x_in, edge, ext, dext, conv_ref, sig_ref, qk_ref,
    ratio_ref, gram_ref, score_ref, solve_ref, base_ref, weight_ref, push_ref,
    a_mine, bc_mine, a_sib, bc_sib, row_a, col_a, cut_out, cut_in, row_bc, tile_out, tile_in,
    state_ref, own_ref, tail_ref, spill_ref, inbox, last_ref,
    gw_ref, gw_sib, gw_row, gw_col, total_ref, glogit_ref, gdecay_ref,
    load_sem, store_sem, own_sem, x_send, x_recv, edge_send, edge_recv, swap_send, swap_recv,
    row_send, row_recv, col_send, col_recv, tile_send, tile_recv,
    spill_send, spill_recv, back_send, back_recv,
):
    me, c = lax.axis_index("head"), lax.axis_index("ctx")
    heads, rows = g_ref.shape
    slab, width = x_hbm.shape[0], x_in.shape[1]
    half = rows // 2
    col_len = nc // (2 * row_len)
    share = DV // row_len
    k_at = lax.rem(c, 2)
    y_at = lax.rem(lax.div(c, 2), row_len)
    x_at = lax.div(c, 2 * row_len)
    low = k_at == 0
    after, before = lax.rem(c + 1, nc), lax.rem(c + nc - 1, nc)
    sibling = ctx_at(c + 1 - 2 * k_at)
    other = ctx_at(lax.rem(c + nc - 1 + 2 * k_at, nc))

    def in_row(y, parity):
        return ctx_at((x_at * row_len + y) * 2 + parity)

    def in_col(x):
        return ctx_at((x * row_len + y_at) * 2 + k_at)

    def row_off(d):
        return lax.rem(y_at + d, row_len)

    def col_off(d):
        return lax.rem(x_at + d, col_len)

    def to_row(kind, d, source, target):
        return remote(
            source, target, row_send.at[kind, d], row_recv.at[kind, y_at], in_row(row_off(d), k_at)
        )

    def from_row(kind, d, buffer):
        y = row_off(d)
        remote(
            buffer.at[y], buffer.at[y], row_send.at[kind, d], row_recv.at[kind, y], in_row(y, k_at)
        ).wait_recv()

    def to_col(kind, d, source, target):
        return remote(
            source, target, col_send.at[kind, d], col_recv.at[kind, x_at], in_col(col_off(d))
        )

    def from_col(kind, d, buffer):
        x = col_off(d)
        remote(
            buffer.at[x], buffer.at[x], col_send.at[kind, d], col_recv.at[kind, x], in_col(x)
        ).wait_recv()

    row_steps, col_steps = range(1, row_len), range(1, col_len)

    loads = [
        pltpu.make_async_copy(source, target, load_sem.at[i])
        for i, (source, target) in enumerate(
            (
                (logit_hbm, logit_ref),
                (g_hbm, g_ref),
                (w_hbm, w_ref),
                (do_hbm, do_ref),
                (first_hbm.at[k_at], start),
                (final_hbm.at[k_at], end),
            )
        )
    ]
    for load in loads:
        load.start()

    def slab_at(z):
        return x_in.at[pl.ds(pl.multiple_of(z * slab, slab), slab), :]

    def cols(z, at=0, size=width):
        return pl.ds(pl.multiple_of(z * width + at, 128), size)

    own = pltpu.make_async_copy(x_hbm.at[:, cols(me)], slab_at(me), own_sem)
    own.start()
    greet(
        [head_at(lax.rem(me + d, n)) for d in far_first(n)]
        + [in_row(row_off(d), k_at) for d in row_steps]
        + [in_row(row_off(d), 1 - k_at) for d in row_steps]
        + [in_col(col_off(d)) for d in col_steps]
        + [sibling, other]
    )

    parts = ((DK, DK), (0, DK), (2 * DK, heads * DV))

    def send_x(i, d):
        at, size = parts[i]
        to = lax.rem(me + d, n)
        return remote(
            x_hbm.at[:, cols(to, at, size)],
            slab_at(me).at[:, pl.ds(at, size)],
            x_send.at[i, d], x_recv.at[i, d], head_at(to),
        )

    def take_x(i, d):
        at, size = parts[i]
        source = lax.rem(me + n - d, n)
        remote(
            x_hbm.at[:, cols(me, at, size)],
            slab_at(source).at[:, pl.ds(at, size)],
            x_send.at[i, d], x_recv.at[i, d], head_at(source),
        ).wait_recv()

    for i in range(3):
        for d in far_first(n):
            send_x(i, d).start()

    def send_edge(i):
        at, size = parts[i]
        return remote(
            x_in.at[pl.ds(rows - EDGE, EDGE), pl.ds(at, size)],
            edge.at[:, pl.ds(at, size)],
            edge_send.at[i], edge_recv.at[i], ctx_at(after),
        )

    for load in loads[:3]:
        load.wait()
    c_row, b_row, wide_cols, i, j = gates(logit_ref, g_ref)

    def col(h):
        return wide_cols[:, h : h + 1]

    def beta(h):
        return wide_cols[:, heads + h : heads + h + 1]

    for h in range(heads):
        ratio_ref[h] = ratios_of(col(h), c_row[h : h + 1, :], i, j)
    last_from = lax.rem(me + 1, n)
    own.wait()

    def convolve(i):
        at, size = parts[i]

        @pl.when(last_from != 0)
        def _():
            take_x(i, last_from)

        send_edge(i).start()
        for d in range(n - 1, 0, -1):

            @pl.when(last_from != d)
            def _():
                take_x(i, d)

        send_edge(i).wait_recv()
        span = slice(at, at + size)
        ext[0:EDGE, span] = jnp.where(c > 0, edge[:, span].astype(f32), 0.0)
        ext[EDGE : EDGE + rows, span] = x_in[:, span].astype(f32)
        conv = w_ref[KW - 1 : KW, span] * ext[EDGE : EDGE + rows, span]
        for tap in range(KW - 1):
            row = EDGE - (KW - 1) + tap
            conv = conv + w_ref[tap : tap + 1, span] * ext[row : row + rows, span]
        sig = 1.0 / (1.0 + jnp.exp(-conv))
        conv_ref[:, span] = conv
        sig_ref[:, span] = sig
        return conv * sig

    b = convolve(0)
    k = b * inv_norm(b)
    qk_ref[:, DK:] = k
    ks = split(k)
    gram = mm(ks, ks, 1, 1)
    lows = []
    for h in range(heads):
        rg = jnp.where(j < i, ratio_ref[h] * gram, 0.0)
        gram_ref[h] = rg
        lows.append(beta(h) * rg)
    diag = []
    for part in lows:
        diag += [part[:half, :half], part[half:, half:]]
    diag = invert_unit_lower(diag, half)
    for h in range(heads):
        one, two = split(diag[2 * h]), split(diag[2 * h + 1])
        corner = mm(split(mm(two, split(lows[h][half:, :half]))), one)
        solve_ref[h, :half, :half] = diag[2 * h]
        solve_ref[h, :half, half:] = jnp.zeros((half, half), f32)
        solve_ref[h, half:, :half] = -corner
        solve_ref[h, half:, half:] = diag[2 * h + 1]
    ii = lax.broadcasted_iota(jnp.int32, (DK, DK), 0)
    jj = lax.broadcasted_iota(jnp.int32, (DK, DK), 1)

    def tail_keys(h):
        return jnp.exp(col(h)[rows - 1 : rows, :] - col(h))

    for h in range(heads):
        weights = mm(split(solve_ref[h]), split((beta(h) * jnp.exp(col(h))) * k))
        weight_ref[h] = weights
        total_decay = jnp.exp(col(h)[rows - 1 : rows, :])
        a_mine[h] = jnp.where(ii == jj, total_decay, 0.0) - mm(
            split(weights), split(tail_keys(h) * k), 0, 0
        )
    swap_a = remote(a_mine, a_sib, swap_send.at[0], swap_recv.at[0], sibling)
    swap_a.start()
    swap_a.wait_recv()
    mine, theirs = a_mine[k_at], a_sib[k_at]
    a1 = split(jnp.where(low, mine, theirs))
    a2 = split(jnp.where(low, theirs, mine))
    row_a[y_at] = mm(a1, a2)

    def row_a_copy(d):
        return to_row(0, d, row_a.at[y_at], row_a.at[y_at])

    for d in row_steps:
        row_a_copy(d).start()

    a = convolve(1)
    q = a * (inv_norm(a) * DK**-0.5)
    qk_ref[:, :DK] = q
    qk = mm(split(q), ks, 1, 1)
    for load in loads[3:]:
        load.wait()
    for h in range(heads):
        score_ref[h] = ratio_ref[h] * qk
        score = split(score_ref[h])
        do = (do_ref[:, h * DV : (h + 1) * DV],)
        reach = jnp.exp(col(h)) * q - mm(score, split(weight_ref[h]))
        bc_mine[h, 1] = mm(do, split(reach), 0, 0)
        push_ref[h] = mm(score, do, 0, 0)
    values = convolve(2)
    for h in range(heads):
        base = mm(split(solve_ref[h]), split(beta(h) * values[:, h * DV : (h + 1) * DV]))
        base_ref[h] = base
        bc_mine[h, 0] = mm(split(base), split(tail_keys(h) * k), 0, 0)
    swap_bc = remote(bc_mine, bc_sib, swap_send.at[1], swap_recv.at[1], sibling)
    swap_bc.start()
    for d in row_steps:
        from_row(0, d, row_a)
    steps = [split(row_a[y]) for y in range(row_len)]
    ahead = {row_len - 2: steps[row_len - 1]}
    for y in range(row_len - 3, -1, -1):
        ahead[y] = split(mm(steps[y + 1], ahead[y + 1]))
    behind = {1: steps[0]}
    for y in range(2, row_len):
        behind[y] = split(mm(behind[y - 1], steps[y - 1]))
    col_a[x_at] = mm(behind[row_len // 2], ahead[row_len // 2 - 1])

    def col_a_copy(d):
        return to_col(0, d, col_a.at[x_at], col_a.at[x_at])

    for d in col_steps:
        col_a_copy(d).start()
    swap_bc.wait_recv()
    mine, theirs = bc_mine[k_at], bc_sib[k_at]
    b1, c1 = jnp.where(low, mine[0], theirs[0]), jnp.where(low, mine[1], theirs[1])
    b2, c2 = jnp.where(low, theirs[0], mine[0]), jnp.where(low, theirs[1], mine[1])
    b12 = mm(split(b1), a2) + b2
    c12 = mm(split(c2), a1, 1, 1) + c1
    cut_out[:, :share, :] = b12.reshape(row_len, share, DK)
    cut_out[:, share:, :] = c12.reshape(row_len, share, DK)

    def cut_copy(d):
        return to_row(1, d, cut_out.at[row_off(d)], cut_in.at[y_at])

    for d in row_steps:
        cut_copy(d).start()
    cut_in[y_at] = cut_out[y_at]
    start[...] = start[...].T
    end[...] = end[...].T
    for d in row_steps:
        from_row(1, d, cut_in)
    gained = {1: cut_in[0, :share, :]}
    owed = {row_len - 2: cut_in[row_len - 1, share:, :]}
    for t in range(1, row_len):
        u = row_len - 1 - t
        gained[t + 1] = mm(split(gained[t]), steps[t]) + cut_in[t, :share, :]
        owed[u - 1] = mm(split(owed[u]), steps[u], 1, 1) + cut_in[u, share:, :]
    row_bc[x_at, :share, :] = gained[row_len]
    row_bc[x_at, share:, :] = owed[-1]

    def row_bc_copy(d):
        return to_col(1, d, row_bc.at[x_at], row_bc.at[x_at])

    for d in col_steps:
        row_bc_copy(d).start()
    my_rows = pl.ds(pl.multiple_of(y_at * share, share), share)
    s, d_state = start[my_rows, :], end[my_rows, :]
    for d in col_steps:
        from_col(0, d, col_a)
    leaps = [split(col_a[x]) for x in range(col_len)]
    for d in col_steps:
        from_col(1, d, row_bc)
    for t in range(col_len - 1):
        u = col_len - 1 - t
        s = jnp.where(t < x_at, mm(split(s), leaps[t]) + row_bc[t, :share, :], s)
        back = mm(split(d_state), leaps[u], 1, 1) + row_bc[u, share:, :]
        d_state = jnp.where(u > x_at, back, d_state)
    ss, ds = split(s), split(d_state)
    for y in range(row_len):
        tile_out[y, :share, :] = mm(ss, behind[y]) + gained[y] if y else s
        tile_out[y, share:, :] = mm(ds, ahead[y], 1, 1) + owed[y] if y < row_len - 1 else d_state

    def tile_copy(d, flip):
        y = row_off(d)
        parity = k_at + flip - 2 * k_at * flip
        return remote(
            tile_out.at[y], tile_in.at[k_at, y_at],
            tile_send.at[flip, d], tile_recv.at[k_at, y_at], in_row(y, parity),
        )

    def tile_wait(d, flip):
        y = row_off(d)
        parity = k_at + flip - 2 * k_at * flip
        remote(
            tile_out.at[y], tile_in.at[parity, y],
            tile_send.at[flip, d], tile_recv.at[parity, y], in_row(y, parity),
        ).wait_recv()

    tile_steps = [(d, flip) for d in row_steps for flip in (0, 1)] + [(0, 1)]
    for d, flip in tile_steps:
        tile_copy(d, flip).start()
    tile_in[k_at, y_at] = tile_out[y_at]
    for d, flip in tile_steps:
        tile_wait(d, flip)
    for h in range(heads):
        s = tile_in[h, :, :share, :].reshape(DV, DK)
        d_state = tile_in[h, :, share:, :].reshape(DV, DK)
        theirs = split(a_sib[h])
        state_ref[h, 0] = jnp.where(low, s, mm(split(s), theirs) + bc_sib[h, 0])
        state_ref[h, 1] = jnp.where(low, mm(split(d_state), theirs, 1, 1) + bc_sib[h, 1], d_state)

    dext[0:EDGE, :] = jnp.zeros((EDGE, width), f32)
    dext[EDGE + rows :, :] = jnp.zeros((dext.shape[0] - EDGE - rows, width), f32)

    def silu_slope(span):
        s = sig_ref[:, span]
        return s * (1.0 + conv_ref[:, span] * (1.0 - s))

    spans = ((2 * DK, heads * DV), (0, 2 * DK))

    def spill_copy(i):
        at, size = spans[i]
        span = pl.ds(at, size)
        return remote(
            spill_ref.at[:, span], inbox.at[:, span],
            spill_send.at[i], spill_recv.at[i], ctx_at(before),
        )

    def send_back(i, d, source=None):
        at, size = spans[i]
        to = lax.rem(me + d, n)
        if source is None:
            source = own_ref.at[pl.ds(pl.multiple_of(to * slab, slab), slab), :]
        return remote(
            source.at[:, pl.ds(at, size)], out_hbm.at[:, cols(me, at, size)],
            back_send.at[i, d], back_recv.at[i, d], head_at(to),
        )

    def unconvolve(i):
        at, size = spans[i]
        span = slice(at, at + size)
        own = w_ref[KW - 1 : KW, span] * dext[EDGE : EDGE + rows, span]
        spill = w_ref[KW - 1 : KW, span] * dext[0:EDGE, span]
        for tap in range(KW - 1):
            back = KW - 1 - tap
            own = own + w_ref[tap : tap + 1, span] * dext[EDGE + back : EDGE + back + rows, span]
            spill = spill + w_ref[tap : tap + 1, span] * dext[back : back + EDGE, span]
        spill_ref[:, span] = spill
        spill_copy(i).start()
        own_ref[:, span] = own.astype(bf16)
        tail_ref[:, span] = own[rows - slab :, :]
        for d in far_first(n):

            @pl.when(lax.rem(me + d, n) != n - 1)
            def _():
                send_back(i, d).start()

    q, k = qk_ref[:, :DK], qk_ref[:, DK:]
    qs, ks = split(q), split(k)
    lower = j < i
    kept = []
    for h in range(heads):
        sts, dsts = split(state_ref[h, 0]), split(state_ref[h, 1])
        tail_k = tail_keys(h) * k
        update = base_ref[h] - mm(split(weight_ref[h]), sts, 1, 1)
        d_update = push_ref[h] + mm(split(tail_k), dsts, 1, 1)
        x = mm(split(solve_ref[h]), split(d_update), 0, 0)
        span = slice(2 * DK + h * DV, 2 * DK + (h + 1) * DV)
        dext[EDGE : EDGE + rows, span] = (beta(h) * x) * silu_slope(span)
        v = conv_ref[:, span] * sig_ref[:, span]
        kept.append((sts, dsts, tail_k, split(update), split(x), jnp.sum(x * v, axis=1, keepdims=True)))
    unconvolve(0)
    dq = None
    row_terms, col_terms = [], []
    for h in range(heads):
        sts, dsts, tail_k, us, xs, xv = kept[h]
        decays = jnp.exp(col(h))
        total_decay = jnp.exp(col(h)[rows - 1 : rows, :])
        ratios = ratio_ref[h]
        score = score_ref[h]
        do = (do_ref[:, h * DV : (h + 1) * DV],)
        d_score = mm(do, us, 1, 1)
        d_low = -mm(xs, us, 1, 1)
        y = -mm(xs, sts)
        d_tail = mm(us, dsts)
        rgd = gram_ref[h] * d_low
        part_q = decays * mm(do, sts)
        part_k = tail_keys(h) * d_tail + (beta(h) * decays) * y
        z = ratios * d_score
        d_gram = jnp.where(lower, beta(h) * (ratios * d_low), 0.0)
        if dq is None:
            dq, dk, zs, dgs = part_q, part_k, z, d_gram
        else:
            dq, dk, zs, dgs = dq + part_q, dk + part_k, zs + z, dgs + d_gram
        flow = jnp.where(lower, score * d_score, 0.0) + beta(h) * rgd
        yk = decays * jnp.sum(y * k, axis=1, keepdims=True)
        tk = jnp.sum(tail_k * d_tail, axis=1, keepdims=True)
        d_beta = xv + yk + jnp.sum(rgd, axis=1, keepdims=True)
        d_cum = (
            jnp.sum(flow, axis=1, keepdims=True)
            + jnp.sum(q * part_q, axis=1, keepdims=True)
            + beta(h) * yk
            - tk
        )
        ends = total_decay * jnp.sum(
            state_ref[h, 0] * state_ref[h, 1], keepdims=True
        ) + jnp.sum(tk, keepdims=True)
        at_end = lax.broadcasted_iota(jnp.int32, (rows, 1), 0) == rows - 1
        col_terms.append((d_cum + jnp.where(at_end, ends, 0.0), d_beta))
        row_terms.append(jnp.sum(flow, axis=0, keepdims=True))
    zs, dgs = split(zs), split(dgs)
    dq = dq + mm(zs, ks)
    dk = dk + mm(zs, qs, 0, 0) + mm(dgs, ks) + mm(dgs, ks, 0, 0)
    for at, d, factor in ((0, dq, DK**-0.5), (DK, dk, 1.0)):
        span = slice(at, at + DK)
        value = conv_ref[:, span] * sig_ref[:, span]
        inv = inv_norm(value)
        inner = jnp.sum(value * d, axis=1, keepdims=True)
        d_act = (inv * factor) * (d - value * (inv * inv * inner))
        dext[EDGE : EDGE + rows, span] = d_act * silu_slope(span)
    unconvolve(1)
    d_conv = dext[EDGE : EDGE + rows, :]
    for tap in range(KW):
        row = EDGE - (KW - 1) + tap
        gw_ref[tap : tap + 1, :] = jnp.sum(d_conv * ext[row : row + rows, :], axis=0, keepdims=True)
    swap_gw = remote(gw_ref, gw_sib, swap_send.at[2], swap_recv.at[2], sibling)
    swap_gw.start()

    for i_part in range(2):
        spill_copy(i_part).wait_recv()
    last_ref[...] = tail_ref[...].astype(bf16)
    more = jnp.where(c < nc - 1, inbox[...], 0.0)
    last_ref[slab - EDGE :, :] = (tail_ref[slab - EDGE :, :] + more).astype(bf16)
    to_last = lax.rem(2 * n - 1 - me, n)
    mine_out = out_hbm.at[:, cols(me)]
    own_back = pltpu.make_async_copy(
        own_ref.at[pl.ds(pl.multiple_of(me * slab, slab), slab), :], mine_out, own_sem
    )
    last_back = pltpu.make_async_copy(last_ref, mine_out, own_sem)

    @pl.when(me != n - 1)
    def _():
        for i_part in range(2):
            send_back(i_part, to_last, last_ref).start()
        own_back.start()

    @pl.when(me == n - 1)
    def _():
        last_back.start()

    swap_gw.wait_recv()
    gw_row[y_at] = jnp.where(low, gw_ref[...], gw_sib[...]) + jnp.where(low, gw_sib[...], gw_ref[...])

    def gw_row_copy(d):
        return to_row(2, d, gw_row.at[y_at], gw_row.at[y_at])

    def gw_col_copy(d):
        return to_col(2, d, gw_col.at[x_at], gw_col.at[x_at])

    for d in row_steps:
        gw_row_copy(d).start()
    lanes = lax.broadcasted_iota(jnp.int32, (rows, 8), 1)
    packed = jnp.zeros((rows, 8), f32)
    for h in range(heads):
        packed = jnp.where(lanes == h, col_terms[h][0], packed)
        packed = jnp.where(lanes == heads + h, col_terms[h][1], packed)
    packed = packed.T
    glogit_ref[...] = packed[heads : 2 * heads] * b_row * (1.0 - b_row)
    d_cum = packed[:heads] - jnp.concatenate(row_terms, axis=0)
    onward = jnp.where(i >= j, 1.0, 0.0).astype(bf16)
    d1 = d_cum.astype(bf16)
    rest = d_cum - d1.astype(f32)
    d2 = rest.astype(bf16)
    d3 = (rest - d2.astype(f32)).astype(bf16)
    gdecay_ref[...] = (dot(d3, onward, 1, 0) + dot(d2, onward, 1, 0)) + dot(d1, onward, 1, 0)
    stores = [
        pltpu.make_async_copy(glogit_ref, glogit_hbm, store_sem.at[0]),
        pltpu.make_async_copy(gdecay_ref, gdecay_hbm, store_sem.at[1]),
        pltpu.make_async_copy(total_ref, total_hbm, store_sem.at[2]),
    ]
    stores[0].start()
    stores[1].start()
    for d in row_steps:
        from_row(2, d, gw_row)
    total = gw_row[0]
    for y in range(1, row_len):
        total = total + gw_row[y]
    gw_col[x_at] = total
    for d in col_steps:
        gw_col_copy(d).start()
    for d in col_steps:
        from_col(2, d, gw_col)
    total = gw_col[0]
    for x in range(1, col_len):
        total = total + gw_col[x]
    total_ref[...] = total
    stores[2].start()

    for i_part in range(3):
        for d in range(1, n):
            send_x(i_part, d).wait_send()
        send_edge(i_part).wait_send()
    for swap in (swap_a, swap_bc, swap_gw):
        swap.wait_send()
    for d in row_steps:
        row_a_copy(d).wait_send()
        cut_copy(d).wait_send()
        gw_row_copy(d).wait_send()
    for d in col_steps:
        col_a_copy(d).wait_send()
        row_bc_copy(d).wait_send()
        gw_col_copy(d).wait_send()
    for d, flip in tile_steps:
        tile_copy(d, flip).wait_send()

    for i_part in range(2):
        at, size = spans[i_part]
        spill_copy(i_part).wait_send()
        for d in range(1, n):
            source = lax.rem(me + n - d, n)
            send_back(i_part, d, last_ref).wait_send()
            remote(
                last_ref.at[:, pl.ds(at, size)], out_hbm.at[:, cols(source, at, size)],
                back_send.at[i_part, d], back_recv.at[i_part, d], head_at(source),
            ).wait_recv()
    last_back.wait()
    for store in stores:
        store.wait()


def settle_kernel(*refs):
    for source, target in zip(refs[:4], refs[4:]):
        target[...] = source[...]


def on_device(mixed_in, conv_weight, logits, decay_log, initial_state, final_state_grad, grad_out):
    n, nc = lax.axis_size("head"), lax.axis_size("ctx")
    heads, rows = decay_log.shape
    slab = mixed_in.shape[0]
    width = mixed_in.shape[1] // n
    row_len = 4
    col_len = nc // (2 * row_len)
    share = DV // row_len
    sems = pltpu.SemaphoreType.DMA
    vm = pltpu.VMEM
    anywhere = pl.BlockSpec(memory_space=pltpu.HBM)
    square = vm((heads, rows, rows), f32)
    tall = vm((heads, rows, DK), f32)
    state = vm((DV, DK), f32)
    results = pl.pallas_call(
        functools.partial(layer_kernel, n, nc, row_len),
        out_shape=(
            shape_of(*mixed_in.shape, dtype=bf16),
            shape_of(*conv_weight.shape),
            shape_of(heads, rows),
            shape_of(heads, rows),
        ),
        in_specs=[anywhere] * 7,
        out_specs=(anywhere,) * 4,
        scratch_shapes=[
            vm((KW, width), f32), vm((heads, rows), f32), vm((heads, rows), f32),
            vm((rows, heads * DV), bf16), state, state,
            vm((rows, width), bf16), vm((EDGE, width), bf16),
            vm((EDGE + rows, width), f32), vm((2 * EDGE + rows, width), f32),
            vm((rows, width), f32), vm((rows, width), f32), vm((rows, 2 * DK), f32),
            square, square, square, square, tall, tall, tall,
            vm((heads, DK, DK), f32), vm((heads, 2, DV, DK), f32),
            vm((heads, DK, DK), f32), vm((heads, 2, DV, DK), f32),
            vm((row_len, DK, DK), f32), vm((col_len, DK, DK), f32),
            vm((row_len, 2 * share, DK), f32), vm((row_len, 2 * share, DK), f32),
            vm((col_len, 2 * share, DK), f32), vm((row_len, 2 * share, DK), f32),
            vm((2, row_len, 2 * share, DK), f32), vm((heads, 2, DV, DK), f32),
            vm((rows, width), bf16), vm((slab, width), f32), vm((EDGE, width), f32),
            vm((EDGE, width), f32), vm((slab, width), bf16),
            vm((KW, width), f32), vm((KW, width), f32),
            vm((row_len, KW, width), f32), vm((col_len, KW, width), f32),
            vm((KW, width), f32), vm((heads, rows), f32), vm((heads, rows), f32),
            sems((6,)), sems((3,)), sems,
            sems((3, n)), sems((3, n)), sems((3,)), sems((3,)), sems((3,)), sems((3,)),
            sems((3, row_len)), sems((3, row_len)), sems((3, col_len)), sems((3, col_len)),
            sems((2, row_len)), sems((2, row_len)),
            sems((2,)), sems((2,)), sems((2, n)), sems((2, n)),
        ],
        compiler_params=pltpu.CompilerParams(
            collective_id=1, has_side_effects=True, vmem_limit_bytes=63 << 20
        ),
        name="layer",
    )(mixed_in, conv_weight, logits, decay_log, grad_out, initial_state, final_state_grad)
    return pl.pallas_call(
        settle_kernel,
        out_shape=tuple(shape_of(*part.shape, dtype=part.dtype) for part in results),
        name="settle",
    )(*results)


def solution(mesh):
    in_specs = (
        P(("ctx", "head"), None),
        P(None, "head"),
        P("head", "ctx"),
        P("head", "ctx"),
        P("head", None, None),
        P("head", None, None),
        P("ctx", "head"),
    )
    out_specs = (P(("ctx", "head"), None), P(None, "head"), P("head", "ctx"), P("head", "ctx"))
    return jax.shard_map(
        on_device, mesh=mesh, in_specs=in_specs, out_specs=out_specs, check_vma=False
    )
```

```python
import functools
import jax
import jax.numpy as jnp
from jax import lax
from jax.experimental import pallas as pl
from jax.experimental.pallas import tpu as pltpu
from jax.sharding import PartitionSpec as P

DK = 128
DV = 128
KW = 4
EDGE = 16

f32 = jnp.float32
bf16 = jnp.bfloat16
norm_eps = 1e-06


def split(a):
    hi = a.astype(bf16)
    return (hi, (a - hi.astype(f32)).astype(bf16))


def dot(a, b, ca, cb):
    return lax.dot_general(a, b, (((ca,), (cb,)), ((), ())), preferred_element_type=f32)


def mm(a, b, ca=1, cb=0):
    out = dot(a[0], b[0], ca, cb)
    if len(b) > 1:
        out = out + dot(a[0], b[1], ca, cb)
    if len(a) > 1:
        out = out + dot(a[1], b[0], ca, cb)
    return out


def inv_norm(a):
    return lax.rsqrt(jnp.sum(a * a, axis=-1, keepdims=True) + norm_eps)


def gates(logit_ref, g_ref):
    heads, rows = g_ref.shape
    i = lax.broadcasted_iota(jnp.int32, (rows, rows), 0)
    j = lax.broadcasted_iota(jnp.int32, (rows, rows), 1)
    upto = jnp.where(i <= j, 1.0, 0.0).astype(bf16)
    g = g_ref[...]
    g1 = g.astype(bf16)
    rest = g - g1.astype(f32)
    g2 = rest.astype(bf16)
    g3 = (rest - g2.astype(f32)).astype(bf16)
    c_row = (dot(g3, upto, 1, 0) + dot(g2, upto, 1, 0)) + dot(g1, upto, 1, 0)
    b_row = 1.0 / (1.0 + jnp.exp(-logit_ref[...]))
    pad = jnp.zeros((8 - 2 * heads, rows), f32)
    cols = jnp.concatenate([c_row, b_row, pad], axis=0).T
    return c_row, b_row, cols, i, j


def ratios_of(c_col, c_row, i, j):
    return jnp.where(j <= i, jnp.exp(jnp.where(j <= i, c_col - c_row, 0.0)), 0.0)


def invert_unit_lower(low, n):
    i = lax.broadcasted_iota(jnp.int32, (n, n), 0)
    j = lax.broadcasted_iota(jnp.int32, (n, n), 1)
    eye = jnp.where(i == j, 1.0, 0.0)
    inv = [eye - jnp.where((i ^ j) == 1, part, 0.0) for part in low]
    shift = 1
    while (1 << shift) < n:
        pick = ((i >> shift) ^ (j >> shift)) == 1
        parts = [split(a) for a in inv]
        mid = [
            mm(p, split(jnp.where(pick, part, 0.0))) for p, part in zip(parts, low)
        ]
        inv = [a - mm(split(m), p) for a, m, p in zip(inv, mid, parts)]
        shift += 1
    return inv


def shape_of(*extent, dtype=f32):
    return jax.ShapeDtypeStruct(extent, dtype)


def ctx_at(i):
    return {"ctx": i}


def head_at(i):
    return {"head": i}


def remote(src, dst, send, recv, device):
    return pltpu.make_async_remote_copy(
        src_ref=src,
        dst_ref=dst,
        send_sem=send,
        recv_sem=recv,
        device_id=device,
        device_id_type=pl.DeviceIdType.MESH,
    )


def greet(devices):
    barrier = pltpu.get_barrier_semaphore()
    for device in devices:
        pl.semaphore_signal(
            barrier, inc=1, device_id=device, device_id_type=pl.DeviceIdType.MESH
        )
    pl.semaphore_wait(barrier, len(devices))


def far_first(n):
    order = []
    for d in range(n // 2, 0, -1):
        order += [d] if 2 * d == n else [d, n - d]
    return order


def layer_kernel(
    n, nc, row_len, x_hbm, w_hbm, logit_hbm, g_hbm, do_hbm, first_hbm, final_hbm,
    out_hbm, total_hbm, glogit_hbm, gdecay_hbm,
    w_ref, logit_ref, g_ref, do_ref, start, end,
    x_in, edge, ext, dext, conv_ref, sig_ref, qk_ref,
    ratio_ref, gram_ref, score_ref, solve_ref, base_ref, weight_ref, push_ref, pull_ref,
    a_mine, bc_mine, a_sib, bc_sib, row_a, col_a, cut_out, cut_in, row_bc, tile_out, tile_in,
    state_ref, own_ref, tail_ref, spill_ref, inbox, last_ref,
    gw_ref, gw_sib, gw_row, gw_col, total_ref, glogit_ref, gdecay_ref,
    load_sem, store_sem, own_sem, x_send, x_recv, edge_send, edge_recv, swap_send, swap_recv,
    row_send, row_recv, col_send, col_recv, tile_send, tile_recv,
    spill_send, spill_recv, back_send, back_recv,
):
    me, c = lax.axis_index("head"), lax.axis_index("ctx")
    heads, rows = g_ref.shape
    slab, width = x_hbm.shape[0], x_in.shape[1]
    half = rows // 2
    col_len = nc // (2 * row_len)
    share = DV // row_len
    k_at = lax.rem(c, 2)
    y_at = lax.rem(lax.div(c, 2), row_len)
    x_at = lax.div(c, 2 * row_len)
    low = k_at == 0
    after, before = lax.rem(c + 1, nc), lax.rem(c + nc - 1, nc)
    sibling = ctx_at(c + 1 - 2 * k_at)
    other = ctx_at(lax.rem(c + nc - 1 + 2 * k_at, nc))

    def in_row(y, parity):
        return ctx_at((x_at * row_len + y) * 2 + parity)

    def in_col(x):
        return ctx_at((x * row_len + y_at) * 2 + k_at)

    def row_off(d):
        return lax.rem(y_at + d, row_len)

    def col_off(d):
        return lax.rem(x_at + d, col_len)

    def to_row(kind, d, source, target):
        return remote(
            source, target, row_send.at[kind, d], row_recv.at[kind, y_at], in_row(row_off(d), k_at)
        )

    def from_row(kind, d, buffer):
        y = row_off(d)
        remote(
            buffer.at[y], buffer.at[y], row_send.at[kind, d], row_recv.at[kind, y], in_row(y, k_at)
        ).wait_recv()

    def to_col(kind, d, source, target):
        return remote(
            source, target, col_send.at[kind, d], col_recv.at[kind, x_at], in_col(col_off(d))
        )

    def from_col(kind, d, buffer):
        x = col_off(d)
        remote(
            buffer.at[x], buffer.at[x], col_send.at[kind, d], col_recv.at[kind, x], in_col(x)
        ).wait_recv()

    row_steps, col_steps = far_first(row_len), far_first(col_len)

    loads = [
        pltpu.make_async_copy(source, target, load_sem.at[i])
        for i, (source, target) in enumerate(
            (
                (logit_hbm, logit_ref),
                (g_hbm, g_ref),
                (w_hbm, w_ref),
                (do_hbm, do_ref),
                (first_hbm.at[k_at], start),
                (final_hbm.at[k_at], end),
            )
        )
    ]
    for load in loads:
        load.start()

    def slab_at(z):
        return x_in.at[pl.ds(pl.multiple_of(z * slab, slab), slab), :]

    def cols(z, at=0, size=width):
        return pl.ds(pl.multiple_of(z * width + at, 128), size)

    own = pltpu.make_async_copy(x_hbm.at[:, cols(me)], slab_at(me), own_sem)
    own.start()
    greet(
        [head_at(lax.rem(me + d, n)) for d in far_first(n)]
        + [in_row(row_off(d), k_at) for d in row_steps]
        + [in_row(row_off(d), 1 - k_at) for d in row_steps]
        + [in_col(col_off(d)) for d in col_steps]
        + [sibling, other]
    )

    parts = ((DK, DK), (0, DK), (2 * DK, heads * DV))

    def send_x(i, d):
        at, size = parts[i]
        to = lax.rem(me + d, n)
        return remote(
            x_hbm.at[:, cols(to, at, size)],
            slab_at(me).at[:, pl.ds(at, size)],
            x_send.at[i, d], x_recv.at[i, d], head_at(to),
        )

    def take_x(i, d):
        at, size = parts[i]
        source = lax.rem(me + n - d, n)
        remote(
            x_hbm.at[:, cols(me, at, size)],
            slab_at(source).at[:, pl.ds(at, size)],
            x_send.at[i, d], x_recv.at[i, d], head_at(source),
        ).wait_recv()

    for i in range(3):
        for d in far_first(n):
            send_x(i, d).start()

    def send_edge(i):
        at, size = parts[i]
        return remote(
            x_in.at[pl.ds(rows - EDGE, EDGE), pl.ds(at, size)],
            edge.at[:, pl.ds(at, size)],
            edge_send.at[i], edge_recv.at[i], ctx_at(after),
        )

    for load in loads[:3]:
        load.wait()
    c_row, b_row, wide_cols, i, j = gates(logit_ref, g_ref)

    def col(h):
        return wide_cols[:, h : h + 1]

    def beta(h):
        return wide_cols[:, heads + h : heads + h + 1]

    for h in range(heads):
        ratio_ref[h] = ratios_of(col(h), c_row[h : h + 1, :], i, j)
    last_from = lax.rem(me + 1, n)
    own.wait()

    def convolve(i):
        at, size = parts[i]

        @pl.when(last_from != 0)
        def _():
            take_x(i, last_from)

        send_edge(i).start()
        for d in range(n - 1, 0, -1):

            @pl.when(last_from != d)
            def _():
                take_x(i, d)

        send_edge(i).wait_recv()
        span = slice(at, at + size)
        ext[0:EDGE, span] = jnp.where(c > 0, edge[:, span].astype(f32), 0.0)
        ext[EDGE : EDGE + rows, span] = x_in[:, span].astype(f32)
        conv = w_ref[KW - 1 : KW, span] * ext[EDGE : EDGE + rows, span]
        for tap in range(KW - 1):
            row = EDGE - (KW - 1) + tap
            conv = conv + w_ref[tap : tap + 1, span] * ext[row : row + rows, span]
        sig = 1.0 / (1.0 + jnp.exp(-conv))
        conv_ref[:, span] = conv
        sig_ref[:, span] = sig
        return conv * sig

    b = convolve(0)
    k = b * inv_norm(b)
    qk_ref[:, DK:] = k
    ks = split(k)
    gram = mm(ks, ks, 1, 1)
    lows = []
    for h in range(heads):
        rg = jnp.where(j < i, ratio_ref[h] * gram, 0.0)
        gram_ref[h] = rg
        lows.append(beta(h) * rg)
    diag = []
    for part in lows:
        diag += [part[:half, :half], part[half:, half:]]
    diag = invert_unit_lower(diag, half)
    for h in range(heads):
        one, two = split(diag[2 * h]), split(diag[2 * h + 1])
        corner = mm(split(mm(two, split(lows[h][half:, :half]))), one)
        solve_ref[h, :half, :half] = diag[2 * h]
        solve_ref[h, :half, half:] = jnp.zeros((half, half), f32)
        solve_ref[h, half:, :half] = -corner
        solve_ref[h, half:, half:] = diag[2 * h + 1]
    ii = lax.broadcasted_iota(jnp.int32, (DK, DK), 0)
    jj = lax.broadcasted_iota(jnp.int32, (DK, DK), 1)

    def tail_keys(h):
        return jnp.exp(col(h)[rows - 1 : rows, :] - col(h))

    for h in range(heads):
        weights = mm(split(solve_ref[h]), split((beta(h) * jnp.exp(col(h))) * k))
        weight_ref[h] = weights
        total_decay = jnp.exp(col(h)[rows - 1 : rows, :])
        a_mine[h] = jnp.where(ii == jj, total_decay, 0.0) - mm(
            split(weights), split(tail_keys(h) * k), 0, 0
        )
    swap_a = remote(a_mine, a_sib, swap_send.at[0], swap_recv.at[0], sibling)
    swap_a.start()
    for h in range(heads):
        pull_ref[h] = mm(split(solve_ref[h]), split(tail_keys(h) * k), 0, 0)
    a = convolve(1)
    q = a * (inv_norm(a) * DK**-0.5)
    qk_ref[:, :DK] = q
    qk = mm(split(q), ks, 1, 1)
    for h in range(heads):
        score_ref[h] = ratio_ref[h] * qk
    swap_a.wait_recv()
    mine, theirs = a_mine[k_at], a_sib[k_at]
    a1 = split(jnp.where(low, mine, theirs))
    a2 = split(jnp.where(low, theirs, mine))
    row_a[y_at] = mm(a1, a2)

    def row_a_copy(d):
        return to_row(0, d, row_a.at[y_at], row_a.at[y_at])

    for d in row_steps:
        row_a_copy(d).start()

    for load in loads[3:]:
        load.wait()
    for h in range(heads):
        do = (do_ref[:, h * DV : (h + 1) * DV],)
        reach = jnp.exp(col(h)) * q - mm(split(score_ref[h]), split(weight_ref[h]))
        bc_mine[h, 1] = mm(do, split(reach), 0, 0)
    values = convolve(2)
    for h in range(heads):
        written = split(beta(h) * values[:, h * DV : (h + 1) * DV])
        bc_mine[h, 0] = mm(written, split(pull_ref[h]), 0, 0)
    swap_bc = remote(bc_mine, bc_sib, swap_send.at[1], swap_recv.at[1], sibling)
    swap_bc.start()
    for d in row_steps:
        from_row(0, d, row_a)
    steps = [split(row_a[y]) for y in range(row_len)]
    ahead = {row_len - 2: steps[row_len - 1]}
    for y in range(row_len - 3, -1, -1):
        ahead[y] = split(mm(steps[y + 1], ahead[y + 1]))
    behind = {1: steps[0]}
    for y in range(2, row_len):
        behind[y] = split(mm(behind[y - 1], steps[y - 1]))
    col_a[x_at] = mm(behind[row_len // 2], ahead[row_len // 2 - 1])

    def col_a_copy(d):
        return to_col(0, d, col_a.at[x_at], col_a.at[x_at])

    for d in col_steps:
        col_a_copy(d).start()
    swap_bc.wait_recv()
    mine, theirs = bc_mine[k_at], bc_sib[k_at]
    b1, c1 = jnp.where(low, mine[0], theirs[0]), jnp.where(low, mine[1], theirs[1])
    b2, c2 = jnp.where(low, theirs[0], mine[0]), jnp.where(low, theirs[1], mine[1])
    b12 = mm(split(b1), a2) + b2
    c12 = mm(split(c2), a1, 1, 1) + c1
    cut_out[:, :share, :] = b12.reshape(row_len, share, DK)
    cut_out[:, share:, :] = c12.reshape(row_len, share, DK)

    def cut_copy(d):
        return to_row(1, d, cut_out.at[row_off(d)], cut_in.at[y_at])

    for d in row_steps:
        cut_copy(d).start()
    cut_in[y_at] = cut_out[y_at]
    start[...] = start[...].T
    end[...] = end[...].T
    for h in range(heads):
        solve = split(solve_ref[h])
        do = (do_ref[:, h * DV : (h + 1) * DV],)
        push_ref[h] = mm(solve, split(mm(split(score_ref[h]), do, 0, 0)), 0, 0)
        base_ref[h] = mm(solve, split(beta(h) * values[:, h * DV : (h + 1) * DV]))
    for d in row_steps:
        from_row(1, d, cut_in)
    gives = [cut_in[y, :share, :] for y in range(row_len)]
    takes = [cut_in[y, share:, :] for y in range(row_len)]
    row_give, row_take = gives[row_len - 1], takes[0]
    for y in range(row_len - 1):
        row_give = row_give + mm(split(gives[y]), ahead[y])
        row_take = row_take + mm(split(takes[y + 1]), behind[y + 1], 1, 1)
    row_bc[x_at, :share, :] = row_give
    row_bc[x_at, share:, :] = row_take

    def row_bc_copy(d):
        return to_col(1, d, row_bc.at[x_at], row_bc.at[x_at])

    for d in col_steps:
        row_bc_copy(d).start()
    gained = {1: gives[0]}
    owed = {row_len - 2: takes[row_len - 1]}
    for t in range(1, row_len - 1):
        u = row_len - 1 - t
        gained[t + 1] = mm(split(gained[t]), steps[t]) + gives[t]
        owed[u - 1] = mm(split(owed[u]), steps[u], 1, 1) + takes[u]
    my_rows = pl.ds(pl.multiple_of(y_at * share, share), share)
    s, d_state = start[my_rows, :], end[my_rows, :]
    for d in col_steps:
        from_col(0, d, col_a)
    leaps = [split(col_a[x]) for x in range(col_len)]
    between = {}
    for t in range(-1, col_len):
        for x in range(t + 2, col_len + 1):
            reach = leaps[x - 1]
            between[t, x] = reach if x == t + 2 else split(mm(between[t, x - 1], reach))

    def pick(choices):
        hi, lo = choices[0][1]
        for x, part in choices[1:]:
            hi = jnp.where(x_at == x, part[0], hi)
            lo = jnp.where(x_at == x, part[1], lo)
        return hi, lo

    def carried(t, value):
        far_rows = [(x, between[t, x]) for x in range(t + 2, col_len)]
        near_term = jnp.where(x_at == t + 1, value, 0.0)
        if not far_rows:
            return near_term
        return jnp.where(x_at > t + 1, mm(split(value), pick(far_rows)), near_term)

    def carried_back(t, value):
        far_rows = [(x, between[x, t]) for x in range(t - 1)]
        near_term = jnp.where(x_at == t - 1, value, 0.0)
        if not far_rows:
            return near_term
        return jnp.where(x_at < t - 1, mm(split(value), pick(far_rows), 1, 1), near_term)

    s, d_state = carried(-1, s), carried_back(col_len, d_state)
    for d in col_steps:
        from_col(1, d, row_bc)
    for t in range(col_len - 1):
        u = col_len - 1 - t
        s = s + carried(t, row_bc[t, :share, :])
        d_state = d_state + carried_back(u, row_bc[u, share:, :])
    ss, ds = split(s), split(d_state)
    for y in range(row_len):
        tile_out[y, :share, :] = mm(ss, behind[y]) + gained[y] if y else s
        tile_out[y, share:, :] = mm(ds, ahead[y], 1, 1) + owed[y] if y < row_len - 1 else d_state

    def tile_copy(d, flip):
        y = row_off(d)
        parity = k_at + flip - 2 * k_at * flip
        return remote(
            tile_out.at[y], tile_in.at[k_at, y_at],
            tile_send.at[flip, d], tile_recv.at[k_at, y_at], in_row(y, parity),
        )

    def tile_wait(d, flip):
        y = row_off(d)
        parity = k_at + flip - 2 * k_at * flip
        remote(
            tile_out.at[y], tile_in.at[parity, y],
            tile_send.at[flip, d], tile_recv.at[parity, y], in_row(y, parity),
        ).wait_recv()

    tile_steps = [(d, flip) for d in row_steps for flip in (0, 1)] + [(0, 1)]
    for d, flip in tile_steps:
        tile_copy(d, flip).start()
    tile_in[k_at, y_at] = tile_out[y_at]
    for d, flip in tile_steps:
        tile_wait(d, flip)
    for h in range(heads):
        s = tile_in[h, :, :share, :].reshape(DV, DK)
        d_state = tile_in[h, :, share:, :].reshape(DV, DK)
        theirs = split(a_sib[h])
        state_ref[h, 0] = jnp.where(low, s, mm(split(s), theirs) + bc_sib[h, 0])
        state_ref[h, 1] = jnp.where(low, mm(split(d_state), theirs, 1, 1) + bc_sib[h, 1], d_state)

    dext[0:EDGE, :] = jnp.zeros((EDGE, width), f32)
    dext[EDGE + rows :, :] = jnp.zeros((dext.shape[0] - EDGE - rows, width), f32)

    def silu_slope(span):
        s = sig_ref[:, span]
        return s * (1.0 + conv_ref[:, span] * (1.0 - s))

    spans = ((2 * DK, heads * DV), (0, 2 * DK))

    def spill_copy(i):
        at, size = spans[i]
        span = pl.ds(at, size)
        return remote(
            spill_ref.at[:, span], inbox.at[:, span],
            spill_send.at[i], spill_recv.at[i], ctx_at(before),
        )

    def send_back(i, d, source=None):
        at, size = spans[i]
        to = lax.rem(me + d, n)
        if source is None:
            source = own_ref.at[pl.ds(pl.multiple_of(to * slab, slab), slab), :]
        return remote(
            source.at[:, pl.ds(at, size)], out_hbm.at[:, cols(me, at, size)],
            back_send.at[i, d], back_recv.at[i, d], head_at(to),
        )

    def unconvolve(i):
        at, size = spans[i]
        span = slice(at, at + size)
        own = w_ref[KW - 1 : KW, span] * dext[EDGE : EDGE + rows, span]
        spill = w_ref[KW - 1 : KW, span] * dext[0:EDGE, span]
        for tap in range(KW - 1):
            back = KW - 1 - tap
            own = own + w_ref[tap : tap + 1, span] * dext[EDGE + back : EDGE + back + rows, span]
            spill = spill + w_ref[tap : tap + 1, span] * dext[back : back + EDGE, span]
        spill_ref[:, span] = spill
        spill_copy(i).start()
        own_ref[:, span] = own.astype(bf16)
        tail_ref[:, span] = own[rows - slab :, :]
        for d in far_first(n):

            @pl.when(lax.rem(me + d, n) != n - 1)
            def _():
                send_back(i, d).start()

    q, k = qk_ref[:, :DK], qk_ref[:, DK:]
    qs, ks = split(q), split(k)
    lower = j < i
    kept = []
    for h in range(heads):
        sts, dsts = split(state_ref[h, 0]), split(state_ref[h, 1])
        tail_k = tail_keys(h) * k
        update = base_ref[h] - mm(split(weight_ref[h]), sts, 1, 1)
        x = push_ref[h] + mm(split(pull_ref[h]), dsts, 1, 1)
        span = slice(2 * DK + h * DV, 2 * DK + (h + 1) * DV)
        dext[EDGE : EDGE + rows, span] = (beta(h) * x) * silu_slope(span)
        kept.append((sts, dsts, tail_k, split(update), x))
    unconvolve(0)
    dq = None
    sides = []
    for h in range(heads):
        sts, dsts, tail_k, us, x = kept[h]
        xs = split(x)
        decays = jnp.exp(col(h))
        ratios = ratio_ref[h]
        do = (do_ref[:, h * DV : (h + 1) * DV],)
        d_score = mm(do, us, 1, 1)
        d_low = -mm(xs, us, 1, 1)
        y = -mm(xs, sts)
        d_tail = mm(us, dsts)
        part_q = decays * mm(do, sts)
        part_k = tail_keys(h) * d_tail + (beta(h) * decays) * y
        z = ratios * d_score
        d_gram = jnp.where(lower, beta(h) * (ratios * d_low), 0.0)
        if dq is None:
            dq, dk, zs, dgs = part_q, part_k, z, d_gram
        else:
            dq, dk, zs, dgs = dq + part_q, dk + part_k, zs + z, dgs + d_gram
        sides.append((d_score, d_low, y, d_tail, part_q))
    zs, dgs = split(zs), split(dgs)
    dq = dq + mm(zs, ks)
    dk = dk + mm(zs, qs, 0, 0) + mm(dgs, ks) + mm(dgs, ks, 0, 0)
    for at, d, factor in ((0, dq, DK**-0.5), (DK, dk, 1.0)):
        span = slice(at, at + DK)
        value = conv_ref[:, span] * sig_ref[:, span]
        inv = inv_norm(value)
        inner = jnp.sum(value * d, axis=1, keepdims=True)
        d_act = (inv * factor) * (d - value * (inv * inv * inner))
        dext[EDGE : EDGE + rows, span] = d_act * silu_slope(span)
    unconvolve(1)
    d_conv = dext[EDGE : EDGE + rows, :]
    for tap in range(KW):
        row = EDGE - (KW - 1) + tap
        gw_ref[tap : tap + 1, :] = jnp.sum(d_conv * ext[row : row + rows, :], axis=0, keepdims=True)
    swap_gw = remote(gw_ref, gw_sib, swap_send.at[2], swap_recv.at[2], sibling)
    swap_gw.start()

    for i_part in range(2):
        spill_copy(i_part).wait_recv()
    last_ref[...] = tail_ref[...].astype(bf16)
    more = jnp.where(c < nc - 1, inbox[...], 0.0)
    last_ref[slab - EDGE :, :] = (tail_ref[slab - EDGE :, :] + more).astype(bf16)
    to_last = lax.rem(2 * n - 1 - me, n)
    mine_out = out_hbm.at[:, cols(me)]
    own_back = pltpu.make_async_copy(
        own_ref.at[pl.ds(pl.multiple_of(me * slab, slab), slab), :], mine_out, own_sem
    )
    last_back = pltpu.make_async_copy(last_ref, mine_out, own_sem)

    @pl.when(me != n - 1)
    def _():
        for i_part in range(2):
            send_back(i_part, to_last, last_ref).start()
        own_back.start()

    @pl.when(me == n - 1)
    def _():
        last_back.start()

    swap_gw.wait_recv()
    gw_row[y_at] = jnp.where(low, gw_ref[...], gw_sib[...]) + jnp.where(low, gw_sib[...], gw_ref[...])

    def gw_row_copy(d):
        return to_row(2, d, gw_row.at[y_at], gw_row.at[y_at])

    def gw_col_copy(d):
        return to_col(2, d, gw_col.at[x_at], gw_col.at[x_at])

    for d in row_steps:
        gw_row_copy(d).start()
    row_terms, col_terms = [], []
    for h in range(heads):
        d_score, d_low, y, d_tail, part_q = sides[h]
        span = slice(2 * DK + h * DV, 2 * DK + (h + 1) * DV)
        tail_k, x = kept[h][2], kept[h][4]
        xv = jnp.sum(x * (conv_ref[:, span] * sig_ref[:, span]), axis=1, keepdims=True)
        total_decay = jnp.exp(col(h)[rows - 1 : rows, :])
        rgd = gram_ref[h] * d_low
        flow = jnp.where(lower, score_ref[h] * d_score, 0.0) + beta(h) * rgd
        yk = jnp.exp(col(h)) * jnp.sum(y * k, axis=1, keepdims=True)
        tk = jnp.sum(tail_k * d_tail, axis=1, keepdims=True)
        d_beta = xv + yk + jnp.sum(rgd, axis=1, keepdims=True)
        d_cum = (
            jnp.sum(flow, axis=1, keepdims=True)
            + jnp.sum(q * part_q, axis=1, keepdims=True)
            + beta(h) * yk
            - tk
        )
        ends = total_decay * jnp.sum(
            state_ref[h, 0] * state_ref[h, 1], keepdims=True
        ) + jnp.sum(tk, keepdims=True)
        at_end = lax.broadcasted_iota(jnp.int32, (rows, 1), 0) == rows - 1
        col_terms.append((d_cum + jnp.where(at_end, ends, 0.0), d_beta))
        row_terms.append(jnp.sum(flow, axis=0, keepdims=True))
    lanes = lax.broadcasted_iota(jnp.int32, (rows, 8), 1)
    packed = jnp.zeros((rows, 8), f32)
    for h in range(heads):
        packed = jnp.where(lanes == h, col_terms[h][0], packed)
        packed = jnp.where(lanes == heads + h, col_terms[h][1], packed)
    packed = packed.T
    glogit_ref[...] = packed[heads : 2 * heads] * b_row * (1.0 - b_row)
    d_cum = packed[:heads] - jnp.concatenate(row_terms, axis=0)
    onward = jnp.where(i >= j, 1.0, 0.0).astype(bf16)
    d1 = d_cum.astype(bf16)
    rest = d_cum - d1.astype(f32)
    d2 = rest.astype(bf16)
    d3 = (rest - d2.astype(f32)).astype(bf16)
    gdecay_ref[...] = (dot(d3, onward, 1, 0) + dot(d2, onward, 1, 0)) + dot(d1, onward, 1, 0)
    stores = [
        pltpu.make_async_copy(glogit_ref, glogit_hbm, store_sem.at[0]),
        pltpu.make_async_copy(gdecay_ref, gdecay_hbm, store_sem.at[1]),
        pltpu.make_async_copy(total_ref, total_hbm, store_sem.at[2]),
    ]
    stores[0].start()
    stores[1].start()
    for d in row_steps:
        from_row(2, d, gw_row)
    total = gw_row[0]
    for y in range(1, row_len):
        total = total + gw_row[y]
    gw_col[x_at] = total
    for d in col_steps:
        gw_col_copy(d).start()
    for d in col_steps:
        from_col(2, d, gw_col)
    total = gw_col[0]
    for x in range(1, col_len):
        total = total + gw_col[x]
    total_ref[...] = total
    stores[2].start()

    for i_part in range(3):
        for d in range(1, n):
            send_x(i_part, d).wait_send()
        send_edge(i_part).wait_send()
    for swap in (swap_a, swap_bc, swap_gw):
        swap.wait_send()
    for d in row_steps:
        row_a_copy(d).wait_send()
        cut_copy(d).wait_send()
        gw_row_copy(d).wait_send()
    for d in col_steps:
        col_a_copy(d).wait_send()
        row_bc_copy(d).wait_send()
        gw_col_copy(d).wait_send()
    for d, flip in tile_steps:
        tile_copy(d, flip).wait_send()

    for i_part in range(2):
        at, size = spans[i_part]
        spill_copy(i_part).wait_send()
        for d in range(1, n):
            source = lax.rem(me + n - d, n)
            send_back(i_part, d, last_ref).wait_send()
            remote(
                last_ref.at[:, pl.ds(at, size)], out_hbm.at[:, cols(source, at, size)],
                back_send.at[i_part, d], back_recv.at[i_part, d], head_at(source),
            ).wait_recv()
    last_back.wait()
    for store in stores:
        store.wait()


def settle_kernel(*refs):
    for source, target in zip(refs[:4], refs[4:]):
        target[...] = source[...]


def on_device(mixed_in, conv_weight, logits, decay_log, initial_state, final_state_grad, grad_out):
    n, nc = lax.axis_size("head"), lax.axis_size("ctx")
    heads, rows = decay_log.shape
    slab = mixed_in.shape[0]
    width = mixed_in.shape[1] // n
    row_len = 4
    col_len = nc // (2 * row_len)
    share = DV // row_len
    sems = pltpu.SemaphoreType.DMA
    vm = pltpu.VMEM
    anywhere = pl.BlockSpec(memory_space=pltpu.HBM)
    square = vm((heads, rows, rows), f32)
    tall = vm((heads, rows, DK), f32)
    state = vm((DV, DK), f32)
    results = pl.pallas_call(
        functools.partial(layer_kernel, n, nc, row_len),
        out_shape=(
            shape_of(*mixed_in.shape, dtype=bf16),
            shape_of(*conv_weight.shape),
            shape_of(heads, rows),
            shape_of(heads, rows),
        ),
        in_specs=[anywhere] * 7,
        out_specs=(anywhere,) * 4,
        scratch_shapes=[
            vm((KW, width), f32), vm((heads, rows), f32), vm((heads, rows), f32),
            vm((rows, heads * DV), bf16), state, state,
            vm((rows, width), bf16), vm((EDGE, width), bf16),
            vm((EDGE + rows, width), f32), vm((2 * EDGE + rows, width), f32),
            vm((rows, width), f32), vm((rows, width), f32), vm((rows, 2 * DK), f32),
            square, square, square, square, tall, tall, tall, tall,
            vm((heads, DK, DK), f32), vm((heads, 2, DV, DK), f32),
            vm((heads, DK, DK), f32), vm((heads, 2, DV, DK), f32),
            vm((row_len, DK, DK), f32), vm((col_len, DK, DK), f32),
            vm((row_len, 2 * share, DK), f32), vm((row_len, 2 * share, DK), f32),
            vm((col_len, 2 * share, DK), f32), vm((row_len, 2 * share, DK), f32),
            vm((2, row_len, 2 * share, DK), f32), vm((heads, 2, DV, DK), f32),
            vm((rows, width), bf16), vm((slab, width), f32), vm((EDGE, width), f32),
            vm((EDGE, width), f32), vm((slab, width), bf16),
            vm((KW, width), f32), vm((KW, width), f32),
            vm((row_len, KW, width), f32), vm((col_len, KW, width), f32),
            vm((KW, width), f32), vm((heads, rows), f32), vm((heads, rows), f32),
            sems((6,)), sems((3,)), sems,
            sems((3, n)), sems((3, n)), sems((3,)), sems((3,)), sems((3,)), sems((3,)),
            sems((3, row_len)), sems((3, row_len)), sems((3, col_len)), sems((3, col_len)),
            sems((2, row_len)), sems((2, row_len)),
            sems((2,)), sems((2,)), sems((2, n)), sems((2, n)),
        ],
        compiler_params=pltpu.CompilerParams(
            collective_id=1, has_side_effects=True, vmem_limit_bytes=63 << 20
        ),
        name="layer",
    )(mixed_in, conv_weight, logits, decay_log, grad_out, initial_state, final_state_grad)
    return pl.pallas_call(
        settle_kernel,
        out_shape=tuple(shape_of(*part.shape, dtype=part.dtype) for part in results),
        name="settle",
    )(*results)


def solution(mesh):
    in_specs = (
        P(("ctx", "head"), None),
        P(None, "head"),
        P("head", "ctx"),
        P("head", "ctx"),
        P("head", None, None),
        P("head", None, None),
        P("ctx", "head"),
    )
    out_specs = (P(("ctx", "head"), None), P(None, "head"), P("head", "ctx"), P("head", "ctx"))
    return jax.shard_map(
        on_device, mesh=mesh, in_specs=in_specs, out_specs=out_specs, check_vma=False
    )
```
